768 devices in a mesh: dp: 96 (over z, x, core), mp: 8 (over y).
Axes of the slice: x: 4, y: 8, z: 12, core: 2. Of those that a mesh axis runs over, the one named last changes fastest.
Arguments:
- partial_grads: bfloat16 [96, 1536, 4096], P('dp', None, 'mp'), may hold values from -1.25 to 1.25
- band_owner: int32 [96], replicated, may hold values from 0 to 95, as said below
- left_factor: float32 [1536, 4096], P('dp', 'mp'), may hold values from -1 to 2.5
- right_factor: float32 [1536, 4096], P('dp', 'mp'), may hold values from -1 to 2.5
- left_root: bfloat16 [1536, 4096], P('dp', 'mp'), may hold values from -1 to 2.5, as said below
- right_root: bfloat16 [1536, 4096], P('dp', 'mp'), may hold values from -1 to 2.5, as said below
Outputs:
- direction: bfloat16 [1536, 4096], P(None, 'mp')
- left_updated: float32 [1536, 4096], P('dp', 'mp')
- right_updated: float32 [1536, 4096], P('dp', 'mp')
The draws below stay inside these ranges and needn't reach their ends.
Inputs may be any that keep to these rules, and one draw needn't show every extreme that they name: `band_owner`: a permutation: every index of dp owns exactly one band. `left_root`: in band order, every 512 x 512 block is symmetric. `right_root`: in band order, every 512 x 512 block is symmetric.
All inputs are finite; a program needn't handle non-finite values.
Results may differ from the reference program's by a relative error of at most 0.01.
Values may be sent and summed in bfloat16 or wider, within the bound.
A program may use at most 32 MiB of HBM per device.

```python
import jax
import jax.numpy as jnp
from jax import lax

BLK = 512
NB = 3
BAND = 16
N_DP = 96
N_MP = 8


def owner_table(key):
    return jax.random.permutation(jax.random.fold_in(key, 101), N_DP).astype(jnp.int32)


def symmetric_bands(key, salt_tag, floor_val, ceiling, spread):
    noise_key = jax.random.fold_in(key, salt_tag)
    diag_key = jax.random.fold_in(key, salt_tag + 1)
    howmany = NB * N_MP
    noise_vals = jnp.clip(jax.random.normal(noise_key, (howmany, BLK, BLK), jnp.float32), -4.0, 4.0)
    symmetric = (noise_vals + jnp.transpose(noise_vals, (0, 2, 1))) * (spread / jnp.sqrt(2.0 * BLK))
    diagonal = jnp.exp(jax.random.uniform(diag_key, (howmany, BLK), jnp.float32, jnp.log(floor_val), jnp.log(ceiling)))
    blocks = symmetric + diagonal[:, :, None] * jnp.eye(BLK, dtype=jnp.float32)[None]
    bands = blocks.reshape(NB, N_MP, BLK, BLK).transpose(0, 2, 1, 3).reshape(N_DP, BAND, N_MP * BLK)
    owners = owner_table(key)
    placed = jnp.zeros((N_DP, BAND, N_MP * BLK), jnp.float32).at[owners].set(bands)
    return placed.reshape(NB * BLK, N_MP * BLK)


def draw_band_owner(key, part):
    return owner_table(key)


def draw_left_factor(key, part):
    return symmetric_bands(key, 11, 0.5, 2.0, 0.25)


def draw_right_factor(key, part):
    return symmetric_bands(key, 21, 0.5, 2.0, 0.25)


def draw_left_root(key, part):
    return symmetric_bands(key, 31, 0.6, 1.8, 0.25).astype(jnp.bfloat16)


def draw_right_root(key, part):
    return symmetric_bands(key, 41, 0.6, 1.8, 0.25).astype(jnp.bfloat16)


def with_spikes(array, rng, source, target, blocks, factor):
    def block_of(position):
        return (jnp.arange(array.shape[position]) // (array.shape[position] // blocks)).reshape((-1,) + (1,) * (array.ndim - 1 - position))

    near = jax.random.permutation(rng, blocks)[block_of(target)]
    other_side = (block_of(target) + blocks // 2) % blocks
    return jnp.where((block_of(source) == near) | (block_of(source) == other_side), factor * array, array)


def block_scale(own_key, dims, cuts, smallest, largest):
    def one(dim, parts):
        heights = jax.random.uniform(jax.random.fold_in(jax.random.fold_in(own_key, 6), dim), (parts,), jnp.float32, smallest / len(cuts), largest / len(cuts))
        return jnp.repeat(jnp.exp(heights), dims[dim] // parts).reshape((-1,) + (1,) * (len(dims) - dim - 1))

    loudness = one(*cuts[0])
    for cut in cuts[1:]:
        loudness = loudness * one(*cut)
    return loudness


def noise_with(rng, extent, deviation, limit, pieces, heavy, kind=jnp.bfloat16):
    array = deviation * jax.random.normal(rng, extent, jnp.float32)
    if pieces:
        array = array * block_scale(rng, extent, pieces, -0.22, 0.18)
    return jnp.clip(with_spikes(array, jax.random.fold_in(rng, 3), *heavy), -limit, limit).astype(kind)


def setup_inputs(seed: int = 0) -> dict:
    key_of = jax.random.split(jax.random.key(seed), 7)
    return {
        "partial_grads": noise_with(key_of[0], (N_DP, NB * BLK, BLK * N_MP), (0.25 * N_DP ** -0.5), 1.25, ((0, 96), (2, 8)), (0, 1, 96, 4.75)),
        "band_owner": draw_band_owner(jax.random.fold_in(key_of[6], 71), 0),
        "left_factor": draw_left_factor(jax.random.fold_in(key_of[6], 71), 0),
        "right_factor": draw_right_factor(jax.random.fold_in(key_of[6], 71), 0),
        "left_root": draw_left_root(jax.random.fold_in(key_of[6], 71), 0),
        "right_root": draw_right_root(jax.random.fold_in(key_of[6], 71), 0),
    }


BETA = 0.95


def to_blocks(matrix):
    return matrix.reshape(NB, BLK, N_MP, BLK).transpose(0, 2, 1, 3)


def from_blocks(blocks):
    return blocks.transpose(0, 2, 1, 3).reshape(NB * BLK, N_MP * BLK)


def reference(partial_grads, band_owner, left_factor, right_factor, left_root, right_root):
    highest = lax.Precision.HIGHEST
    owners = band_owner.astype(jnp.int32)
    inverse = jnp.argsort(owners).astype(jnp.int32)

    def to_bands(stored):
        return stored.reshape(N_DP, BAND, N_MP * BLK)[owners].reshape(NB * BLK, N_MP * BLK)

    def to_devices(stored):
        return stored.reshape(N_DP, BAND, N_MP * BLK)[inverse].reshape(NB * BLK, N_MP * BLK)

    gradient = jnp.sum(partial_grads, axis=0, dtype=jnp.float32)
    grad16 = gradient.astype(jnp.bfloat16)
    gblocks = to_blocks(grad16).astype(jnp.float32)
    left_term = jnp.einsum('bmik,bmjk->bmij', gblocks, gblocks, precision=highest)
    right_term = jnp.einsum('bmki,bmkj->bmij', gblocks, gblocks, precision=highest)
    left_next = BETA * to_blocks(to_bands(left_factor)) + (1.0 - BETA) * left_term
    right_next = BETA * to_blocks(to_bands(right_factor)) + (1.0 - BETA) * right_term
    left_pre = to_blocks(to_bands(left_root)).astype(jnp.float32)
    right_pre = to_blocks(to_bands(right_root)).astype(jnp.float32)
    mixed = jnp.einsum('bmik,bmkj->bmij', gblocks, right_pre, precision=highest).astype(jnp.bfloat16)
    direction = jnp.einsum('bmik,bmkj->bmij', left_pre, mixed.astype(jnp.float32), precision=highest).astype(jnp.bfloat16)
    left_updated = to_devices(from_blocks(left_next))
    right_updated = to_devices(from_blocks(right_next))
    return from_blocks(direction), left_updated, right_updated
```

```python
import functools

import jax
import jax.numpy as jnp
from jax import lax
from jax.experimental import pallas as pl
from jax.experimental.pallas import tpu as pltpu
from jax.sharding import PartitionSpec as P

BETA = 0.95
NZ, NX, NC = 12, 4, 2
BAND = 16
BLK = 512
NB = 3
ROWS = NB * BLK
HALF = ROWS // NC
QUARTER = HALF // NX
EIGHTH = QUARTER // 2
MESH = pl.DeviceIdType.MESH
F32 = jnp.float32
BF16 = jnp.bfloat16
NEAR = [1, 11, 2, 10, 3, 9, 4, 8, 5, 7, 6]


def exchange(
    grad, left, right, g, p,
    r0, sb, ra, rb, rl, rr, qf, qb, rz, s1, s3,
    sem_local, c_send, c_recv, x_send, x_recv, z_send, z_recv,
    gz_send, gz_recv, gx_send, gx_recv, gc_send, gc_recv,
    px_send, px_recv, pz_send, pz_recv, pc_send, pc_recv,
):
    me = lax.axis_index("dp")
    c = lax.rem(me, NC)
    x = lax.rem(me // NC, NX)
    z = me // (NC * NX)

    def at(zz, xx, cc):
        return (zz * NX + xx) * NC + cc

    def up_x(k):
        return lax.rem(x + k, NX)

    def up_z(k):
        return lax.rem(z + k, NZ)

    partner = at(z, x, 1 - c)
    xp, xm = at(z, up_x(1), c), at(z, up_x(3), c)
    zp, zm = at(up_z(1), x, c), at(up_z(NZ - 1), x, c)
    pending = []

    def copy(src, dst, ss, rs, dev):
        return pltpu.make_async_remote_copy(
            src_ref=src, dst_ref=dst, send_sem=ss, recv_sem=rs,
            device_id={"dp": dev}, device_id_type=MESH,
        )

    def send(*args):
        made = copy(*args)
        made.start()
        pending.append(made)

    def arrived(dst, ss, rs, dev):
        copy(dst, dst, ss, rs, dev).wait_recv()

    barrier = pltpu.get_barrier_semaphore()
    others = [partner] + [at(z, up_x(k), c) for k in (1, 2, 3)]
    others += [at(up_z(k), x, c) for k in NEAR]
    for dev in others:
        pl.semaphore_signal(barrier, inc=1, device_id={"dp": dev}, device_id_type=MESH)

    slot = p.at[c, z, x]
    own = [
        pltpu.make_async_copy(left, slot.at[0], sem_local.at[0]),
        pltpu.make_async_copy(right, slot.at[1], sem_local.at[1]),
    ]
    for one in own:
        one.start()
    for one in own:
        one.wait()
    pl.semaphore_wait(barrier, len(others))

    def rows(start, size):
        return pl.ds(pl.multiple_of(start, BAND), size)

    for r in (2, 1, 3, 0):
        send(
            grad.at[0, rows((1 - c) * HALF + up_x(r) * QUARTER, QUARTER)],
            r0.at[r], c_send.at[r], c_recv.at[r], partner,
        )
    for k in (1, 2, 3):
        send(slot, slot, px_send.at[k], px_recv.at[k], at(z, up_x(k), c))

    def pair_sum(r):
        arrived(r0.at[r], c_send.at[r], c_recv.at[r], partner)
        mine = grad[0, rows(c * HALF + up_x(r) * QUARTER, QUARTER), :].astype(F32)
        return mine + r0[r].astype(F32)

    lo, hi = pl.ds(0, EIGHTH), pl.ds(EIGHTH, EIGHTH)
    sb[2] = pair_sum(2).astype(BF16)
    send(sb.at[2, lo], ra, x_send.at[0], x_recv.at[0], xp)
    send(sb.at[2, hi], rb, x_send.at[1], x_recv.at[1], xm)
    total = pair_sum(1)
    s1[...] = total[:EIGHTH]
    sb[1, hi] = total[EIGHTH:].astype(BF16)
    send(sb.at[1, hi], rl.at[hi], x_send.at[2], x_recv.at[2], xp)
    total = pair_sum(3)
    s3[...] = total[EIGHTH:]
    sb[3, lo] = total[:EIGHTH].astype(BF16)
    send(sb.at[3, lo], rr.at[lo], x_send.at[3], x_recv.at[3], xm)
    qf[...] = pair_sum(0)

    for k in (1, 2, 3):
        there = p.at[c, z, up_x(NX - k)]
        arrived(there, px_send.at[k], px_recv.at[k], xp)

    def plane(zz):
        return p.at[c, zz]

    def bands_on(step):
        if step > 1:
            for way, from_z in ((0, up_z(NZ + 1 - step)), (1, up_z(step - 1))):
                arrived(plane(from_z), pz_send.at[way, step - 1], pz_recv.at[way, step - 1], zp)
        if step <= 6:
            send(plane(up_z(NZ + 1 - step)), plane(up_z(NZ + 1 - step)),
                 pz_send.at[0, step], pz_recv.at[0, step], zp)
        if step <= 5:
            send(plane(up_z(step - 1)), plane(up_z(step - 1)),
                 pz_send.at[1, step], pz_recv.at[1, step], zm)
        for way, from_z in ((0, up_z(NZ + 1 - step)), (1, up_z(step - 1))):
            if way == 0 or step > 1:
                send(plane(from_z), plane(from_z),
                     pc_send.at[way, step], pc_recv.at[way, step], partner)

    bands_on(1)

    arrived(ra, x_send.at[0], x_recv.at[0], xm)
    sb[1, lo] = (s1[...] + ra[...].astype(F32)).astype(BF16)
    send(sb.at[1, lo], rl.at[lo], x_send.at[4], x_recv.at[4], xp)
    arrived(rb, x_send.at[1], x_recv.at[1], xp)
    sb[3, hi] = (s3[...] + rb[...].astype(F32)).astype(BF16)
    send(sb.at[3, hi], rr.at[hi], x_send.at[5], x_recv.at[5], xm)

    bands_on(2)

    arrived(rl.at[hi], x_send.at[2], x_recv.at[2], xm)
    arrived(rr.at[lo], x_send.at[3], x_recv.at[3], xp)
    arrived(rl.at[lo], x_send.at[4], x_recv.at[4], xm)
    arrived(rr.at[hi], x_send.at[5], x_recv.at[5], xp)
    total = qf[...] + rl[...].astype(F32) + rr[...].astype(F32)
    qf[...] = total
    qb[...] = total.astype(BF16)

    for d in reversed(NEAR):
        send(qb.at[rows(up_z(d) * BAND, BAND)], rz.at[d], z_send.at[d], z_recv.at[d],
             at(up_z(d), x, c))

    bands_on(3)

    for d in NEAR:
        arrived(rz.at[d], z_send.at[d], z_recv.at[d], zm)
    total = qf[rows(z * BAND, BAND), :]
    for d in NEAR:
        total = total + rz[d].astype(F32)

    def chunk(xx, zz):
        return g.at[rows((c * NX * NZ + xx * NZ + zz) * BAND, BAND)]

    g[rows((c * NX * NZ + x * NZ + z) * BAND, BAND), :] = total.astype(BF16)

    for d in reversed(NEAR):
        send(chunk(x, z), chunk(x, z), gz_send.at[d], gz_recv.at[d], at(up_z(d), x, c))

    bands_on(4)

    def from_z(d):
        return up_z(NZ - d)

    order = [0] + NEAR
    lag = 3
    for i in range(NZ + lag):
        if i < NZ:
            d = order[i]
            here = chunk(x, from_z(d))
            if d:
                arrived(here, gz_send.at[d], gz_recv.at[d], zm)
            send(here, here, gx_send.at[0, d], gx_recv.at[0, d], xp)
            send(here, here, gx_send.at[1, d], gx_recv.at[1, d], xm)
        if i == NZ - 1:
            mine = g.at[rows((c * NX + x) * QUARTER, QUARTER)]
            send(mine, mine, gc_send.at[0], gc_recv.at[0], partner)
        if i >= lag:
            d = order[i - lag]
            below, above = chunk(up_x(3), from_z(d)), chunk(up_x(1), from_z(d))
            arrived(below, gx_send.at[0, d], gx_recv.at[0, d], xm)
            if d % 2 == 0:
                send(below, below, gx_send.at[2, d], gx_recv.at[2, d], xp)
            arrived(above, gx_send.at[1, d], gx_recv.at[1, d], xp)
            if d % 2 == 1:
                send(above, above, gx_send.at[2, d], gx_recv.at[2, d], xm)
        if i == 5:
            bands_on(5)
        if i == 11:
            bands_on(6)
    for k, r in ((1, 1), (2, 3)):
        part = g.at[rows((c * NX + up_x(r)) * QUARTER, QUARTER)]
        send(part, part, gc_send.at[k], gc_recv.at[k], partner)
    for d in order:
        arrived(chunk(up_x(2), from_z(d)), gx_send.at[2, d], gx_recv.at[2, d], xp)
    part = g.at[rows((c * NX + up_x(2)) * QUARTER, QUARTER)]
    send(part, part, gc_send.at[3], gc_recv.at[3], partner)

    last = plane(up_z(6))
    arrived(last, pz_send.at[0, 6], pz_recv.at[0, 6], zm)
    send(last, last, pc_send.at[0, 7], pc_recv.at[0, 7], partner)

    for k, r in ((0, 0), (1, 1), (2, 3), (3, 2)):
        part = g.at[rows(((1 - c) * NX + up_x(r)) * QUARTER, QUARTER)]
        arrived(part, gc_send.at[k], gc_recv.at[k], partner)
    for step in range(1, 8):
        for way, zz in ((0, up_z(NZ + 1 - step)), (1, up_z(step - 1))):
            if (way == 0 or step > 1) and not (way == 1 and step == 7):
                arrived(p.at[1 - c, zz], pc_send.at[way, step], pc_recv.at[way, step], partner)
    for made in pending:
        made.wait_send()


def gather_all(grad, left, right):
    vmem = pl.BlockSpec(memory_space=pltpu.VMEM)
    dma = pltpu.SemaphoreType.DMA
    return pl.pallas_call(
        exchange,
        out_shape=(
            jax.ShapeDtypeStruct((ROWS, BLK), BF16),
            jax.ShapeDtypeStruct((NC, NZ, NX, 2, BAND, BLK), BF16),
        ),
        in_specs=[vmem] * 3,
        out_specs=(vmem, vmem),
        scratch_shapes=[
            pltpu.VMEM((NX, QUARTER, BLK), BF16),
            pltpu.VMEM((NX, QUARTER, BLK), BF16),
            pltpu.VMEM((EIGHTH, BLK), BF16),
            pltpu.VMEM((EIGHTH, BLK), BF16),
            pltpu.VMEM((QUARTER, BLK), BF16),
            pltpu.VMEM((QUARTER, BLK), BF16),
            pltpu.VMEM((QUARTER, BLK), F32),
            pltpu.VMEM((QUARTER, BLK), BF16),
            pltpu.VMEM((NZ, BAND, BLK), BF16),
            pltpu.VMEM((EIGHTH, BLK), F32),
            pltpu.VMEM((EIGHTH, BLK), F32),
            dma((2,)),
            dma((NX,)), dma((NX,)),
            dma((6,)), dma((6,)),
            dma((NZ,)), dma((NZ,)),
            dma((NZ,)), dma((NZ,)),
            dma((3, NZ)), dma((3, NZ)),
            dma((NX,)), dma((NX,)),
            dma((NX,)), dma((NX,)),
            dma((2, 7)), dma((2, 7)),
            dma((2, 8)), dma((2, 8)),
        ],
        compiler_params=pltpu.CompilerParams(
            collective_id=0, has_side_effects=True, vmem_limit_bytes=40 << 20
        ),
    )(grad, left, right)


def dots(owner, g, p, left_factor, right_factor, direction, left_out, right_out, pls, prs):
    me = lax.axis_index("dp")

    def place(k, own):
        d = owner[k]
        cc, xx, zz = lax.rem(d, NC), lax.rem(d // NC, NX), d // (NC * NX)
        at = pl.ds(pl.multiple_of(k * BAND, BAND), BAND)
        pls[at, :] = p[cc, zz, xx, 0]
        prs[at, :] = p[cc, zz, xx, 1]
        return jnp.where(d == me, k, own)

    own = lax.fori_loop(0, NZ * NX * NC, place, jnp.int32(0), unroll=8)
    start = own * BAND
    block = start // BLK
    within = start - block * BLK
    row = g[pl.ds(pl.multiple_of(start, BAND), BAND), :]
    gb = g[pl.ds(pl.multiple_of(block * BLK, BLK), BLK), :]
    last = (((1,), (1,)), ((), ()))
    left_term = lax.dot_general(row, gb, last, preferred_element_type=F32)
    left_out[...] = BETA * left_factor[...] + (1.0 - BETA) * left_term
    which = lax.broadcasted_iota(jnp.int32, (BAND, BLK), 1)
    this = lax.broadcasted_iota(jnp.int32, (BAND, BLK), 0) + within
    onehot = jnp.where(which == this, 1.0, 0.0).astype(BF16)
    column = lax.dot_general(onehot, gb, last, preferred_element_type=F32).astype(BF16)
    right_term = jnp.dot(column, gb, preferred_element_type=F32)
    right_out[...] = BETA * right_factor[...] + (1.0 - BETA) * right_term
    for b in range(NB):
        at = pl.ds(b * BLK, BLK)
        mixed = jnp.dot(g[at, :], prs[at, :], preferred_element_type=F32).astype(BF16)
        direction[at, :] = jnp.dot(pls[at, :], mixed, preferred_element_type=F32).astype(BF16)


def precondition(owner, g, p, left_factor, right_factor):
    vmem = pl.BlockSpec(memory_space=pltpu.VMEM)
    return pl.pallas_call(
        dots,
        out_shape=(
            jax.ShapeDtypeStruct((ROWS, BLK), BF16),
            jax.ShapeDtypeStruct((BAND, BLK), F32),
            jax.ShapeDtypeStruct((BAND, BLK), F32),
        ),
        in_specs=[pl.BlockSpec(memory_space=pltpu.SMEM)] + [vmem] * 4,
        out_specs=(vmem, vmem, vmem),
        scratch_shapes=[pltpu.VMEM((ROWS, BLK), BF16), pltpu.VMEM((ROWS, BLK), BF16)],
        compiler_params=pltpu.CompilerParams(vmem_limit_bytes=40 << 20),
    )(owner, g, p, left_factor, right_factor)


def shards(partial_grads, band_owner, left_factor, right_factor, left_root, right_root):
    g, p = gather_all(partial_grads, left_root, right_root)
    return precondition(band_owner, g, p, left_factor, right_factor)


def solution(mesh):
    placed = (P("dp", None, "mp"), P(), P("dp", "mp"), P("dp", "mp"), P("dp", "mp"), P("dp", "mp"))
    return jax.shard_map(
        shards,
        mesh=mesh,
        in_specs=placed,
        out_specs=(P(None, "mp"), P("dp", "mp"), P("dp", "mp")),
        check_vma=False,
    )
```

```python
import functools

import jax
import jax.numpy as jnp
from jax import lax
from jax.experimental import pallas as pl
from jax.experimental.pallas import tpu as pltpu
from jax.sharding import PartitionSpec as P

BETA = 0.95
NZ, NX, NC = 12, 4, 2
BAND = 16
BLK = 512
NB = 3
ROWS = NB * BLK
HALF = ROWS // NC
QUARTER = HALF // NX
EIGHTH = QUARTER // 2
MESH = pl.DeviceIdType.MESH
F32 = jnp.float32
BF16 = jnp.bfloat16
NEAR = [1, 11, 2, 10, 3, 9, 4, 8, 5, 7, 6]


def exchange(
    grad, left, right, g, p,
    half, r0, sb, ra, rb, rl, rr, qf, qb, rz, s1, s3,
    sem_local, c_send, c_recv, x_send, x_recv, z_send, z_recv,
    gz_send, gz_recv, gx_send, gx_recv, gc_send, gc_recv,
    px_send, px_recv, pz_send, pz_recv, pc_send, pc_recv,
):
    me = lax.axis_index("dp")
    c = lax.rem(me, NC)
    x = lax.rem(me // NC, NX)
    z = me // (NC * NX)

    def at(zz, xx, cc):
        return (zz * NX + xx) * NC + cc

    def up_x(k):
        return lax.rem(x + k, NX)

    def up_z(k):
        return lax.rem(z + k, NZ)

    partner = at(z, x, 1 - c)
    xp, xm = at(z, up_x(1), c), at(z, up_x(3), c)
    zp, zm = at(up_z(1), x, c), at(up_z(NZ - 1), x, c)
    pending = []

    def copy(src, dst, ss, rs, dev):
        return pltpu.make_async_remote_copy(
            src_ref=src, dst_ref=dst, send_sem=ss, recv_sem=rs,
            device_id={"dp": dev}, device_id_type=MESH,
        )

    def send(*args):
        made = copy(*args)
        made.start()
        pending.append(made)

    def arrived(dst, ss, rs, dev):
        copy(dst, dst, ss, rs, dev).wait_recv()

    barrier = pltpu.get_barrier_semaphore()
    others = [partner] + [at(z, up_x(k), c) for k in (1, 2, 3)]
    others += [at(up_z(k), x, c) for k in NEAR]
    for dev in others:
        pl.semaphore_signal(barrier, inc=1, device_id={"dp": dev}, device_id_type=MESH)

    def rows(start, size):
        return pl.ds(pl.multiple_of(start, BAND), size)

    slot = p.at[c, x, z]
    own = [
        pltpu.make_async_copy(left, slot.at[0], sem_local.at[0]),
        pltpu.make_async_copy(right, slot.at[1], sem_local.at[1]),
    ]
    loads = {
        r: pltpu.make_async_copy(
            grad.at[0, rows(c * HALF + up_x(r) * QUARTER, QUARTER)], half.at[r], sem_local.at[2 + r]
        )
        for r in (2, 1, 3, 0)
    }
    for one in own + list(loads.values()):
        one.start()
    pl.semaphore_wait(barrier, len(others))

    for r in (2, 1, 3, 0):
        send(
            grad.at[0, rows((1 - c) * HALF + up_x(r) * QUARTER, QUARTER)],
            r0.at[r], c_send.at[r], c_recv.at[r], partner,
        )
    for one in own:
        one.wait()
    for d in reversed(NEAR):
        send(slot, slot, pz_send.at[d], pz_recv.at[d], at(up_z(d), x, c))

    def pair_sum(r):
        loads[r].wait()
        arrived(r0.at[r], c_send.at[r], c_recv.at[r], partner)
        return half[r].astype(F32) + r0[r].astype(F32)

    lo, hi = pl.ds(0, EIGHTH), pl.ds(EIGHTH, EIGHTH)
    sb[2] = pair_sum(2).astype(BF16)
    send(sb.at[2, lo], ra, x_send.at[0], x_recv.at[0], xp)
    send(sb.at[2, hi], rb, x_send.at[1], x_recv.at[1], xm)
    total = pair_sum(1)
    s1[...] = total[:EIGHTH]
    sb[1, hi] = total[EIGHTH:].astype(BF16)
    send(sb.at[1, hi], rl.at[hi], x_send.at[2], x_recv.at[2], xp)
    total = pair_sum(3)
    s3[...] = total[EIGHTH:]
    sb[3, lo] = total[:EIGHTH].astype(BF16)
    send(sb.at[3, lo], rr.at[lo], x_send.at[3], x_recv.at[3], xm)
    qf[...] = pair_sum(0)

    arrived(ra, x_send.at[0], x_recv.at[0], xm)
    sb[1, lo] = (s1[...] + ra[...].astype(F32)).astype(BF16)
    send(sb.at[1, lo], rl.at[lo], x_send.at[4], x_recv.at[4], xp)
    arrived(rb, x_send.at[1], x_recv.at[1], xp)
    sb[3, hi] = (s3[...] + rb[...].astype(F32)).astype(BF16)
    send(sb.at[3, hi], rr.at[hi], x_send.at[5], x_recv.at[5], xm)


    arrived(rl.at[hi], x_send.at[2], x_recv.at[2], xm)
    arrived(rr.at[lo], x_send.at[3], x_recv.at[3], xp)
    arrived(rl.at[lo], x_send.at[4], x_recv.at[4], xm)
    arrived(rr.at[hi], x_send.at[5], x_recv.at[5], xp)
    total = qf[...] + rl[...].astype(F32) + rr[...].astype(F32)
    qf[...] = total
    qb[...] = total.astype(BF16)

    for d in reversed(NEAR):
        send(qb.at[rows(up_z(d) * BAND, BAND)], rz.at[d], z_send.at[d], z_recv.at[d],
             at(up_z(d), x, c))


    def from_z(d):
        return up_z(NZ - d)

    def bands(r, k=None):
        return p.at[c, up_x(r)] if k is None else p.at[c, up_x(r), pl.ds(k * (NZ // 2), NZ // 2)]

    def pass_bands(r, k, i, dev):
        send(bands(r, k), bands(r, k), px_send.at[i, k], px_recv.at[i, k], dev)

    def give_bands(r, i):
        send(bands(r), bands(r), pc_send.at[i], pc_recv.at[i], partner)

    for d in NEAR:
        arrived(p.at[c, x, from_z(d)], pz_send.at[d], pz_recv.at[d], zm)
    pass_bands(0, 0, 0, xp)
    pass_bands(0, 1, 1, xm)
    pass_bands(0, 1, 0, xp)
    pass_bands(0, 0, 1, xm)
    give_bands(0, 0)

    for d in NEAR:
        arrived(rz.at[d], z_send.at[d], z_recv.at[d], zm)
    total = qf[rows(z * BAND, BAND), :]
    for d in NEAR:
        total = total + rz[d].astype(F32)

    def chunk(xx, zz):
        return g.at[rows((c * NX * NZ + xx * NZ + zz) * BAND, BAND)]

    g[rows((c * NX * NZ + x * NZ + z) * BAND, BAND), :] = total.astype(BF16)

    own_chunk = chunk(x, z)
    for d in reversed(NEAR):
        send(own_chunk, own_chunk, gz_send.at[d], gz_recv.at[d], at(up_z(d), x, c))
    arrived(bands(3, 0), px_send.at[0, 0], px_recv.at[0, 0], xm)
    pass_bands(3, 0, 2, xp)
    arrived(bands(1, 1), px_send.at[1, 1], px_recv.at[1, 1], xp)
    pass_bands(1, 1, 2, xm)
    arrived(bands(3, 1), px_send.at[0, 1], px_recv.at[0, 1], xm)
    give_bands(3, 1)
    arrived(bands(1, 0), px_send.at[1, 0], px_recv.at[1, 0], xp)
    give_bands(1, 2)
    for d in NEAR:
        arrived(chunk(x, from_z(d)), gz_send.at[d], gz_recv.at[d], zm)

    arrived(bands(2, 0), px_send.at[2, 0], px_recv.at[2, 0], xm)
    arrived(bands(2, 1), px_send.at[2, 1], px_recv.at[2, 1], xp)
    give_bands(2, 3)
    def part(r, a, n):
        return g.at[rows((c * NX + up_x(r)) * QUARTER + a, n)]

    mine = part(0, 0, QUARTER)
    lo_half, hi_half = part(0, 0, EIGHTH), part(0, EIGHTH, EIGHTH)
    send(lo_half, lo_half, gx_send.at[0, 0], gx_recv.at[0, 0], xp)
    send(hi_half, hi_half, gx_send.at[1, 1], gx_recv.at[1, 1], xm)
    send(hi_half, hi_half, gx_send.at[0, 1], gx_recv.at[0, 1], xp)
    send(lo_half, lo_half, gx_send.at[1, 0], gx_recv.at[1, 0], xm)
    send(mine, mine, gc_send.at[0, 0], gc_recv.at[0, 0], partner)
    below, above = part(3, 0, EIGHTH), part(1, EIGHTH, EIGHTH)
    arrived(below, gx_send.at[0, 0], gx_recv.at[0, 0], xm)
    send(below, below, gx_send.at[2, 0], gx_recv.at[2, 0], xp)
    arrived(above, gx_send.at[1, 1], gx_recv.at[1, 1], xp)
    send(above, above, gx_send.at[2, 1], gx_recv.at[2, 1], xm)
    arrived(part(3, EIGHTH, EIGHTH), gx_send.at[0, 1], gx_recv.at[0, 1], xm)
    send(part(3, 0, QUARTER), part(3, 0, QUARTER), gc_send.at[1, 0], gc_recv.at[1, 0], partner)
    arrived(part(1, 0, EIGHTH), gx_send.at[1, 0], gx_recv.at[1, 0], xp)
    send(part(1, 0, QUARTER), part(1, 0, QUARTER), gc_send.at[2, 0], gc_recv.at[2, 0], partner)
    arrived(part(2, 0, EIGHTH), gx_send.at[2, 0], gx_recv.at[2, 0], xm)
    arrived(part(2, EIGHTH, EIGHTH), gx_send.at[2, 1], gx_recv.at[2, 1], xp)
    send(part(2, 0, QUARTER), part(2, 0, QUARTER), gc_send.at[3, 0], gc_recv.at[3, 0], partner)

    for k, r in ((0, 0), (1, 3), (2, 1), (3, 2)):
        theirs = g.at[rows(((1 - c) * NX + up_x(r)) * QUARTER, QUARTER)]
        arrived(theirs, gc_send.at[k, 0], gc_recv.at[k, 0], partner)
    for i, r in ((0, 0), (1, 3), (2, 1), (3, 2)):
        arrived(p.at[1 - c, up_x(r)], pc_send.at[i], pc_recv.at[i], partner)
    for made in pending:
        made.wait_send()


def gather_all(grad, left, right):
    vmem = pl.BlockSpec(memory_space=pltpu.VMEM)
    dma = pltpu.SemaphoreType.DMA
    return pl.pallas_call(
        exchange,
        out_shape=(
            jax.ShapeDtypeStruct((ROWS, BLK), BF16),
            jax.ShapeDtypeStruct((NC, NX, NZ, 2, BAND, BLK), BF16),
        ),
        in_specs=[pl.BlockSpec(memory_space=pltpu.HBM)] * 3,
        out_specs=(vmem, vmem),
        scratch_shapes=[
            pltpu.VMEM((NX, QUARTER, BLK), BF16),
            pltpu.VMEM((NX, QUARTER, BLK), BF16),
            pltpu.VMEM((NX, QUARTER, BLK), BF16),
            pltpu.VMEM((EIGHTH, BLK), BF16),
            pltpu.VMEM((EIGHTH, BLK), BF16),
            pltpu.VMEM((QUARTER, BLK), BF16),
            pltpu.VMEM((QUARTER, BLK), BF16),
            pltpu.VMEM((QUARTER, BLK), F32),
            pltpu.VMEM((QUARTER, BLK), BF16),
            pltpu.VMEM((NZ, BAND, BLK), BF16),
            pltpu.VMEM((EIGHTH, BLK), F32),
            pltpu.VMEM((EIGHTH, BLK), F32),
            dma((2 + NX,)),
            dma((NX,)), dma((NX,)),
            dma((6,)), dma((6,)),
            dma((NZ,)), dma((NZ,)),
            dma((NZ,)), dma((NZ,)),
            dma((3, NZ)), dma((3, NZ)),
            dma((NX, NZ)), dma((NX, NZ)),
            dma((3, 2)), dma((3, 2)),
            dma((NZ,)), dma((NZ,)),
            dma((NX,)), dma((NX,)),
        ],
        compiler_params=pltpu.CompilerParams(
            collective_id=0, has_side_effects=True, vmem_limit_bytes=40 << 20
        ),
    )(grad, left, right)


def dots(owner, g, p, left_factor, right_factor, direction, left_out, right_out, pls, prs):
    me = lax.axis_index("dp")

    def place(k, own):
        d = owner[k]
        cc, xx, zz = lax.rem(d, NC), lax.rem(d // NC, NX), d // (NC * NX)
        at = pl.ds(pl.multiple_of(k * BAND, BAND), BAND)
        pls[at, :] = p[cc, xx, zz, 0]
        prs[at, :] = p[cc, xx, zz, 1]
        return jnp.where(d == me, k, own)

    own = lax.fori_loop(0, NZ * NX * NC, place, jnp.int32(0), unroll=8)
    start = own * BAND
    block = start // BLK
    within = start - block * BLK
    row = g[pl.ds(pl.multiple_of(start, BAND), BAND), :]
    gb = g[pl.ds(pl.multiple_of(block * BLK, BLK), BLK), :]
    last = (((1,), (1,)), ((), ()))
    left_term = lax.dot_general(row, gb, last, preferred_element_type=F32)
    left_out[...] = BETA * left_factor[...] + (1.0 - BETA) * left_term
    which = lax.broadcasted_iota(jnp.int32, (BAND, BLK), 1)
    this = lax.broadcasted_iota(jnp.int32, (BAND, BLK), 0) + within
    onehot = jnp.where(which == this, 1.0, 0.0).astype(BF16)
    column = lax.dot_general(onehot, gb, last, preferred_element_type=F32).astype(BF16)
    right_term = jnp.dot(column, gb, preferred_element_type=F32)
    right_out[...] = BETA * right_factor[...] + (1.0 - BETA) * right_term
    for b in range(NB):
        at = pl.ds(b * BLK, BLK)
        mixed = jnp.dot(g[at, :], prs[at, :], preferred_element_type=F32).astype(BF16)
        direction[at, :] = jnp.dot(pls[at, :], mixed, preferred_element_type=F32).astype(BF16)


def precondition(owner, g, p, left_factor, right_factor):
    vmem = pl.BlockSpec(memory_space=pltpu.VMEM)
    return pl.pallas_call(
        dots,
        out_shape=(
            jax.ShapeDtypeStruct((ROWS, BLK), BF16),
            jax.ShapeDtypeStruct((BAND, BLK), F32),
            jax.ShapeDtypeStruct((BAND, BLK), F32),
        ),
        in_specs=[pl.BlockSpec(memory_space=pltpu.SMEM)] + [vmem] * 4,
        out_specs=(vmem, vmem, vmem),
        scratch_shapes=[pltpu.VMEM((ROWS, BLK), BF16), pltpu.VMEM((ROWS, BLK), BF16)],
        compiler_params=pltpu.CompilerParams(vmem_limit_bytes=40 << 20),
    )(owner, g, p, left_factor, right_factor)


def shards(partial_grads, band_owner, left_factor, right_factor, left_root, right_root):
    g, p = gather_all(partial_grads, left_root, right_root)
    return precondition(band_owner, g, p, left_factor, right_factor)


def solution(mesh):
    placed = (P("dp", None, "mp"), P(), P("dp", "mp"), P("dp", "mp"), P("dp", "mp"), P("dp", "mp"))
    return jax.shard_map(
        shards,
        mesh=mesh,
        in_specs=placed,
        out_specs=(P(None, "mp"), P("dp", "mp"), P("dp", "mp")),
        check_vma=False,
    )
```

```python
import functools

import jax
import jax.numpy as jnp
from jax import lax
from jax.experimental import pallas as pl
from jax.experimental.pallas import tpu as pltpu
from jax.sharding import PartitionSpec as P

BETA = 0.95
NZ, NX, NC = 12, 4, 2
BAND = 16
BLK = 512
NB = 3
ROWS = NB * BLK
HALF = ROWS // NC
QUARTER = HALF // NX
EIGHTH = QUARTER // 2
MESH = pl.DeviceIdType.MESH
F32 = jnp.float32
BF16 = jnp.bfloat16
NEAR = [1, 11, 2, 10, 3, 9, 4, 8, 5, 7, 6]


def exchange(
    owner, grad, left, right, g, pls, prs,
    p, half, r0, sb, ra, rb, rl, rr, qf, qb, rz, s1, s3,
    sem_local, c_send, c_recv, x_send, x_recv, z_send, z_recv,
    gz_send, gz_recv, gx_send, gx_recv, gc_send, gc_recv,
    px_send, px_recv, pz_send, pz_recv, pc_send, pc_recv,
):
    me = lax.axis_index("dp")
    c = lax.rem(me, NC)
    x = lax.rem(me // NC, NX)
    z = me // (NC * NX)

    def at(zz, xx, cc):
        return (zz * NX + xx) * NC + cc

    def up_x(k):
        return lax.rem(x + k, NX)

    def up_z(k):
        return lax.rem(z + k, NZ)

    partner = at(z, x, 1 - c)
    xp, xm = at(z, up_x(1), c), at(z, up_x(3), c)
    zp, zm = at(up_z(1), x, c), at(up_z(NZ - 1), x, c)
    pending = []

    def copy(src, dst, ss, rs, dev):
        return pltpu.make_async_remote_copy(
            src_ref=src, dst_ref=dst, send_sem=ss, recv_sem=rs,
            device_id={"dp": dev}, device_id_type=MESH,
        )

    def send(*args):
        made = copy(*args)
        made.start()
        pending.append(made)

    def arrived(dst, ss, rs, dev):
        copy(dst, dst, ss, rs, dev).wait_recv()

    barrier = pltpu.get_barrier_semaphore()
    others = [partner] + [at(z, up_x(k), c) for k in (1, 2, 3)]
    others += [at(up_z(k), x, c) for k in NEAR]
    for dev in others:
        pl.semaphore_signal(barrier, inc=1, device_id={"dp": dev}, device_id_type=MESH)

    def rows(start, size):
        return pl.ds(pl.multiple_of(start, BAND), size)

    slot = p.at[c, x, z]
    own = [
        pltpu.make_async_copy(left, slot.at[0], sem_local.at[0]),
        pltpu.make_async_copy(right, slot.at[1], sem_local.at[1]),
    ]
    loads = {
        r: pltpu.make_async_copy(
            grad.at[0, rows(c * HALF + up_x(r) * QUARTER, QUARTER)], half.at[r], sem_local.at[2 + r]
        )
        for r in (2, 1, 3, 0)
    }
    for one in own + list(loads.values()):
        one.start()
    pl.semaphore_wait(barrier, len(others))

    for r in (2, 1, 3, 0):
        send(
            grad.at[0, rows((1 - c) * HALF + up_x(r) * QUARTER, QUARTER)],
            r0.at[r], c_send.at[r], c_recv.at[r], partner,
        )
    for one in own:
        one.wait()
    def from_z(d):
        return up_z(NZ - d)

    def band_along(d, k):
        band = p.at[c, x, from_z(d)]
        to = (d + k) % NZ
        send(band, band, pz_send.at[to], pz_recv.at[to], at(up_z(k % NZ), x, c))

    for k in (3, -3, 2, -2, 1, -1):
        band_along(0, k)

    far = list(range(4, 9))
    near = list(range(9, 12)) + list(range(0, 4))
    far_lo, far_hi = pl.ds(0, 3 * BAND), pl.ds(3 * BAND, 2 * BAND)
    near_lo, near_hi = pl.ds(5 * BAND, 4 * BAND), pl.ds(9 * BAND, 3 * BAND)
    all_far, all_near = pl.ds(0, 5 * BAND), pl.ds(5 * BAND, 7 * BAND)

    def pair_landed(r):
        loads[r].wait()
        arrived(r0.at[r], c_send.at[r], c_recv.at[r], partner)

    def pair_sum(r, ds):
        return jnp.concatenate(
            [half[r, rows(up_z(d) * BAND, BAND), :].astype(F32)
             + r0[r, rows(up_z(d) * BAND, BAND), :].astype(F32) for d in ds],
            axis=0,
        )

    def begin(i, ds, lo, hi):
        if i == 0:
            pair_landed(2)
        total = pair_sum(2, ds).astype(BF16)
        cut = lo.size
        sb[2, lo], sb[2, hi] = total[:cut], total[cut:]
        send(sb.at[2, lo], ra.at[lo], x_send.at[0, i], x_recv.at[0, i], xp)
        send(sb.at[2, hi], rb.at[hi], x_send.at[1, i], x_recv.at[1, i], xm)
        if i == 0:
            pair_landed(1)
        total = pair_sum(1, ds)
        s1[lo] = total[:cut]
        sb[1, hi] = total[cut:].astype(BF16)
        send(sb.at[1, hi], rl.at[hi], x_send.at[2, i], x_recv.at[2, i], xp)
        if i == 0:
            pair_landed(3)
        total = pair_sum(3, ds)
        s3[hi] = total[cut:]
        sb[3, lo] = total[:cut].astype(BF16)
        send(sb.at[3, lo], rr.at[lo], x_send.at[3, i], x_recv.at[3, i], xm)

    def middle(i, lo, hi):
        arrived(ra.at[lo], x_send.at[0, i], x_recv.at[0, i], xm)
        sb[1, lo] = (s1[lo, :] + ra[lo, :].astype(F32)).astype(BF16)
        send(sb.at[1, lo], rl.at[lo], x_send.at[4, i], x_recv.at[4, i], xp)
        arrived(rb.at[hi], x_send.at[1, i], x_recv.at[1, i], xp)
        sb[3, hi] = (s3[hi, :] + rb[hi, :].astype(F32)).astype(BF16)
        send(sb.at[3, hi], rr.at[hi], x_send.at[5, i], x_recv.at[5, i], xm)

    def finish(i, lo, hi, both, ds):
        arrived(rl.at[hi], x_send.at[2, i], x_recv.at[2, i], xm)
        arrived(rr.at[lo], x_send.at[3, i], x_recv.at[3, i], xp)
        arrived(rl.at[lo], x_send.at[4, i], x_recv.at[4, i], xm)
        arrived(rr.at[hi], x_send.at[5, i], x_recv.at[5, i], xp)
        total = qf[both, :] + rl[both, :].astype(F32) + rr[both, :].astype(F32)
        qf[both] = total
        qb[both] = total.astype(BF16)
        for d in ds:
            send(qb.at[pl.ds((d + 8) % NZ * BAND, BAND)], rz.at[d], z_send.at[d], z_recv.at[d],
                 at(up_z(d), x, c))

    begin(0, far, far_lo, far_hi)
    begin(1, near, near_lo, near_hi)
    pair_landed(0)
    qf[...] = pair_sum(0, far + near)
    for d in (3, 9):
        arrived(p.at[c, x, from_z(d)], pz_send.at[d], pz_recv.at[d], zm)
    over = 3 - 6 * c
    band = p.at[c, x, lax.rem(z - over + NZ, NZ)]
    send(band, band, pz_send.at[6], pz_recv.at[6], at(lax.rem(z + over + NZ, NZ), x, c))
    for k in (2, 1):
        band_along(3, k)
        band_along(9, -k)
    middle(0, far_lo, far_hi)
    middle(1, near_lo, near_hi)
    finish(0, far_lo, far_hi, all_far, (6, 5, 7, 4, 8))
    finish(1, near_lo, near_hi, all_near, (3, 9, 2, 10, 1, 11))

    def bands(r, k=None):
        return p.at[c, up_x(r)] if k is None else p.at[c, up_x(r), pl.ds(k * (NZ // 2), NZ // 2)]

    def pass_bands(r, k, i, dev):
        send(bands(r, k), bands(r, k), px_send.at[i, k], px_recv.at[i, k], dev)

    def give_bands(r, i):
        send(bands(r), bands(r), pc_send.at[i], pc_recv.at[i], partner)

    for d in (1, 11, 2, 10, 4, 8, 5, 7, 6):
        arrived(p.at[c, x, from_z(d)], pz_send.at[d], pz_recv.at[d], zm)
    pass_bands(0, 0, 0, xp)
    pass_bands(0, 1, 1, xm)
    pass_bands(0, 1, 0, xp)
    pass_bands(0, 0, 1, xm)
    give_bands(0, 0)

    for d in NEAR:
        arrived(rz.at[d], z_send.at[d], z_recv.at[d], zm)
    total = qf[8 * BAND : 9 * BAND, :]
    for d in NEAR:
        total = total + rz[d].astype(F32)

    def chunk(xx, zz):
        return g.at[rows((c * NX * NZ + xx * NZ + zz) * BAND, BAND)]

    g[rows((c * NX * NZ + x * NZ + z) * BAND, BAND), :] = total.astype(BF16)

    own_chunk = chunk(x, z)
    for d in reversed(NEAR):
        send(own_chunk, own_chunk, gz_send.at[d], gz_recv.at[d], at(up_z(d), x, c))
    arrived(bands(3, 0), px_send.at[0, 0], px_recv.at[0, 0], xm)
    pass_bands(3, 0, 2, xp)
    arrived(bands(1, 1), px_send.at[1, 1], px_recv.at[1, 1], xp)
    pass_bands(1, 1, 2, xm)
    arrived(bands(3, 1), px_send.at[0, 1], px_recv.at[0, 1], xm)
    give_bands(3, 1)
    arrived(bands(1, 0), px_send.at[1, 0], px_recv.at[1, 0], xp)
    give_bands(1, 2)
    for d in NEAR:
        arrived(chunk(x, from_z(d)), gz_send.at[d], gz_recv.at[d], zm)

    def part(r, a, n):
        return g.at[rows((c * NX + up_x(r)) * QUARTER + a, n)]

    mine = part(0, 0, QUARTER)
    lo_half, hi_half = part(0, 0, EIGHTH), part(0, EIGHTH, EIGHTH)
    send(lo_half, lo_half, gx_send.at[0, 0], gx_recv.at[0, 0], xp)
    send(hi_half, hi_half, gx_send.at[1, 1], gx_recv.at[1, 1], xm)
    send(hi_half, hi_half, gx_send.at[0, 1], gx_recv.at[0, 1], xp)
    send(lo_half, lo_half, gx_send.at[1, 0], gx_recv.at[1, 0], xm)
    send(mine, mine, gc_send.at[0, 0], gc_recv.at[0, 0], partner)
    below, above = part(3, 0, EIGHTH), part(1, EIGHTH, EIGHTH)
    arrived(below, gx_send.at[0, 0], gx_recv.at[0, 0], xm)
    send(below, below, gx_send.at[2, 0], gx_recv.at[2, 0], xp)
    arrived(above, gx_send.at[1, 1], gx_recv.at[1, 1], xp)
    send(above, above, gx_send.at[2, 1], gx_recv.at[2, 1], xm)
    arrived(part(3, EIGHTH, EIGHTH), gx_send.at[0, 1], gx_recv.at[0, 1], xm)
    send(part(3, 0, QUARTER), part(3, 0, QUARTER), gc_send.at[1, 0], gc_recv.at[1, 0], partner)
    arrived(part(1, 0, EIGHTH), gx_send.at[1, 0], gx_recv.at[1, 0], xp)
    send(part(1, 0, QUARTER), part(1, 0, QUARTER), gc_send.at[2, 0], gc_recv.at[2, 0], partner)
    arrived(bands(2, 0), px_send.at[2, 0], px_recv.at[2, 0], xm)
    arrived(bands(2, 1), px_send.at[2, 1], px_recv.at[2, 1], xp)
    give_bands(2, 3)
    for i, r in ((0, 0), (1, 3), (2, 1), (3, 2)):
        arrived(p.at[1 - c, up_x(r)], pc_send.at[i], pc_recv.at[i], partner)

    def place(k, _):
        d = owner[k]
        cc, xx, zz = lax.rem(d, NC), lax.rem(d // NC, NX), d // (NC * NX)
        there = rows(k * BAND, BAND)
        pls[there, :] = p[cc, xx, zz, 0]
        prs[there, :] = p[cc, xx, zz, 1]
        return 0

    lax.fori_loop(0, NZ * NX * NC, place, 0, unroll=8)

    arrived(part(2, 0, EIGHTH), gx_send.at[2, 0], gx_recv.at[2, 0], xm)
    arrived(part(2, EIGHTH, EIGHTH), gx_send.at[2, 1], gx_recv.at[2, 1], xp)
    send(part(2, 0, QUARTER), part(2, 0, QUARTER), gc_send.at[3, 0], gc_recv.at[3, 0], partner)

    for k, r in ((0, 0), (1, 3), (2, 1), (3, 2)):
        theirs = g.at[rows(((1 - c) * NX + up_x(r)) * QUARTER, QUARTER)]
        arrived(theirs, gc_send.at[k, 0], gc_recv.at[k, 0], partner)
    for made in pending:
        made.wait_send()


def gather_all(owner, grad, left, right):
    vmem = pl.BlockSpec(memory_space=pltpu.VMEM)
    dma = pltpu.SemaphoreType.DMA
    return pl.pallas_call(
        exchange,
        out_shape=(
            jax.ShapeDtypeStruct((ROWS, BLK), BF16),
            jax.ShapeDtypeStruct((ROWS, BLK), BF16),
            jax.ShapeDtypeStruct((ROWS, BLK), BF16),
        ),
        in_specs=[pl.BlockSpec(memory_space=pltpu.SMEM)] + [pl.BlockSpec(memory_space=pltpu.HBM)] * 3,
        out_specs=(vmem, vmem, vmem),
        scratch_shapes=[
            pltpu.VMEM((NC, NX, NZ, 2, BAND, BLK), BF16),
            pltpu.VMEM((NX, QUARTER, BLK), BF16),
            pltpu.VMEM((NX, QUARTER, BLK), BF16),
            pltpu.VMEM((NX, QUARTER, BLK), BF16),
            pltpu.VMEM((QUARTER, BLK), BF16),
            pltpu.VMEM((QUARTER, BLK), BF16),
            pltpu.VMEM((QUARTER, BLK), BF16),
            pltpu.VMEM((QUARTER, BLK), BF16),
            pltpu.VMEM((QUARTER, BLK), F32),
            pltpu.VMEM((QUARTER, BLK), BF16),
            pltpu.VMEM((NZ, BAND, BLK), BF16),
            pltpu.VMEM((QUARTER, BLK), F32),
            pltpu.VMEM((QUARTER, BLK), F32),
            dma((2 + NX,)),
            dma((NX,)), dma((NX,)),
            dma((6, 2)), dma((6, 2)),
            dma((NZ,)), dma((NZ,)),
            dma((NZ,)), dma((NZ,)),
            dma((3, NZ)), dma((3, NZ)),
            dma((NX, NZ)), dma((NX, NZ)),
            dma((3, 2)), dma((3, 2)),
            dma((NZ,)), dma((NZ,)),
            dma((NX,)), dma((NX,)),
        ],
        compiler_params=pltpu.CompilerParams(
            collective_id=0, has_side_effects=True, vmem_limit_bytes=40 << 20
        ),
    )(owner, grad, left, right)


def dots(owner, g, pls, prs, left_factor, right_factor, direction, left_out, right_out):
    me = lax.axis_index("dp")

    def find(k, own):
        return jnp.where(owner[k] == me, k, own)

    own = lax.fori_loop(0, NZ * NX * NC, find, jnp.int32(0), unroll=8)
    start = own * BAND
    block = start // BLK
    within = start - block * BLK
    row = g[pl.ds(pl.multiple_of(start, BAND), BAND), :]
    gb = g[pl.ds(pl.multiple_of(block * BLK, BLK), BLK), :]
    last = (((1,), (1,)), ((), ()))
    left_term = lax.dot_general(row, gb, last, preferred_element_type=F32)
    left_out[...] = BETA * left_factor[...] + (1.0 - BETA) * left_term
    which = lax.broadcasted_iota(jnp.int32, (BAND, BLK), 1)
    this = lax.broadcasted_iota(jnp.int32, (BAND, BLK), 0) + within
    onehot = jnp.where(which == this, 1.0, 0.0).astype(BF16)
    column = lax.dot_general(onehot, gb, last, preferred_element_type=F32).astype(BF16)
    right_term = jnp.dot(column, gb, preferred_element_type=F32)
    right_out[...] = BETA * right_factor[...] + (1.0 - BETA) * right_term
    for b in range(NB):
        at = pl.ds(b * BLK, BLK)
        mixed = jnp.dot(g[at, :], prs[at, :], preferred_element_type=F32).astype(BF16)
        direction[at, :] = jnp.dot(pls[at, :], mixed, preferred_element_type=F32).astype(BF16)


def precondition(owner, g, pls, prs, left_factor, right_factor):
    vmem = pl.BlockSpec(memory_space=pltpu.VMEM)
    return pl.pallas_call(
        dots,
        out_shape=(
            jax.ShapeDtypeStruct((ROWS, BLK), BF16),
            jax.ShapeDtypeStruct((BAND, BLK), F32),
            jax.ShapeDtypeStruct((BAND, BLK), F32),
        ),
        in_specs=[pl.BlockSpec(memory_space=pltpu.SMEM)] + [vmem] * 5,
        out_specs=(vmem, vmem, vmem),
        compiler_params=pltpu.CompilerParams(vmem_limit_bytes=40 << 20),
    )(owner, g, pls, prs, left_factor, right_factor)


def shards(partial_grads, band_owner, left_factor, right_factor, left_root, right_root):
    held = [pltpu.with_memory_space_constraint(v, pltpu.HBM) for v in (band_owner, partial_grads, left_root, right_root)]
    g, pls, prs = gather_all(*held)
    return precondition(band_owner, g, pls, prs, left_factor, right_factor)


def solution(mesh):
    placed = (P("dp", None, "mp"), P(), P("dp", "mp"), P("dp", "mp"), P("dp", "mp"), P("dp", "mp"))
    return jax.shard_map(
        shards,
        mesh=mesh,
        in_specs=placed,
        out_specs=(P(None, "mp"), P("dp", "mp"), P("dp", "mp")),
        check_vma=False,
    )
```

```python
import functools

import jax
import jax.numpy as jnp
from jax import lax
from jax.experimental import pallas as pl
from jax.experimental.pallas import tpu as pltpu
from jax.sharding import PartitionSpec as P

BETA = 0.95
NZ, NX, NC = 12, 4, 2
BAND = 16
BLK = 512
NB = 3
ROWS = NB * BLK
HALF = ROWS // NC
QUARTER = HALF // NX
EIGHTH = QUARTER // 2
MESH = pl.DeviceIdType.MESH
F32 = jnp.float32
BF16 = jnp.bfloat16
NEAR = [1, 11, 2, 10, 3, 9, 4, 8, 5, 7, 6]


def exchange(
    owner, grad, left, right, g, pls, prs,
    p, half, r0, sb, ra, rb, rl, rr, qf, qb, rz, s1, s3,
    sem_local, c_send, c_recv, x_send, x_recv, z_send, z_recv,
    gz_send, gz_recv, gx_send, gx_recv, gy_send, gy_recv, gc_send, gc_recv, go_send, go_recv,
    px_send, px_recv, pz_send, pz_recv, pc_send, pc_recv,
):
    me = lax.axis_index("dp")
    c = lax.rem(me, NC)
    x = lax.rem(me // NC, NX)
    z = me // (NC * NX)

    def at(zz, xx, cc):
        return (zz * NX + xx) * NC + cc

    def up_x(k):
        return lax.rem(x + k, NX)

    def up_z(k):
        return lax.rem(z + k, NZ)

    partner = at(z, x, 1 - c)
    xp, xm = at(z, up_x(1), c), at(z, up_x(3), c)
    zp, zm = at(up_z(1), x, c), at(up_z(NZ - 1), x, c)
    pending = []

    def copy(src, dst, ss, rs, dev):
        return pltpu.make_async_remote_copy(
            src_ref=src, dst_ref=dst, send_sem=ss, recv_sem=rs,
            device_id={"dp": dev}, device_id_type=MESH,
        )

    def send(*args):
        made = copy(*args)
        made.start()
        pending.append(made)

    def arrived(dst, ss, rs, dev):
        copy(dst, dst, ss, rs, dev).wait_recv()

    barrier = pltpu.get_barrier_semaphore()
    others = [partner] + [at(z, up_x(k), c) for k in (1, 2, 3)]
    others += [at(up_z(k), x, c) for k in NEAR]
    for dev in others:
        pl.semaphore_signal(barrier, inc=1, device_id={"dp": dev}, device_id_type=MESH)

    def rows(start, size):
        return pl.ds(pl.multiple_of(start, BAND), size)

    slot = p.at[c, x, z]
    own = [
        pltpu.make_async_copy(left, slot.at[0], sem_local.at[0]),
        pltpu.make_async_copy(right, slot.at[1], sem_local.at[1]),
    ]
    loads = {
        r: pltpu.make_async_copy(
            grad.at[c, :, up_x(r)], half.at[r], sem_local.at[2 + r]
        )
        for r in (2, 1, 3, 0)
    }
    for one in own + list(loads.values()):
        one.start()
    pl.semaphore_wait(barrier, len(others))

    for r in (2, 1, 3, 0):
        send(
            grad.at[1 - c, :, up_x(r)],
            r0.at[r], c_send.at[r], c_recv.at[r], partner,
        )
    for one in own:
        one.wait()
    def from_z(d):
        return up_z(NZ - d)

    def band_along(d, k):
        band = p.at[c, x, from_z(d)]
        to = (d + k) % NZ
        send(band, band, pz_send.at[to], pz_recv.at[to], at(up_z(k % NZ), x, c))

    for k in (3, -3, 2, -2, 1, -1):
        band_along(0, k)

    far = list(range(4, 9))
    near = list(range(9, 12)) + list(range(0, 4))
    far_lo, far_hi = pl.ds(0, 3 * BAND), pl.ds(3 * BAND, 2 * BAND)
    near_lo, near_hi = pl.ds(5 * BAND, 4 * BAND), pl.ds(9 * BAND, 3 * BAND)
    all_far, all_near = pl.ds(0, 5 * BAND), pl.ds(5 * BAND, 7 * BAND)

    def pair_landed(r):
        loads[r].wait()
        arrived(r0.at[r], c_send.at[r], c_recv.at[r], partner)

    def pair_sum(r, ds):
        return jnp.concatenate(
            [half[r, up_z(d)].astype(F32) + r0[r, up_z(d)].astype(F32) for d in ds],
            axis=0,
        )

    def begin(i, ds, lo, hi):
        if i == 0:
            pair_landed(2)
        total = pair_sum(2, ds).astype(BF16)
        cut = lo.size
        sb[2, lo], sb[2, hi] = total[:cut], total[cut:]
        send(sb.at[2, lo], ra.at[lo], x_send.at[0, i], x_recv.at[0, i], xp)
        send(sb.at[2, hi], rb.at[hi], x_send.at[1, i], x_recv.at[1, i], xm)
        if i == 0:
            pair_landed(1)
        total = pair_sum(1, ds)
        s1[lo] = total[:cut]
        sb[1, hi] = total[cut:].astype(BF16)
        send(sb.at[1, hi], rl.at[hi], x_send.at[2, i], x_recv.at[2, i], xp)
        if i == 0:
            pair_landed(3)
        total = pair_sum(3, ds)
        s3[hi] = total[cut:]
        sb[3, lo] = total[:cut].astype(BF16)
        send(sb.at[3, lo], rr.at[lo], x_send.at[3, i], x_recv.at[3, i], xm)

    def middle(i, lo, hi):
        arrived(ra.at[lo], x_send.at[0, i], x_recv.at[0, i], xm)
        sb[1, lo] = (s1[lo, :] + ra[lo, :].astype(F32)).astype(BF16)
        send(sb.at[1, lo], rl.at[lo], x_send.at[4, i], x_recv.at[4, i], xp)
        arrived(rb.at[hi], x_send.at[1, i], x_recv.at[1, i], xp)
        sb[3, hi] = (s3[hi, :] + rb[hi, :].astype(F32)).astype(BF16)
        send(sb.at[3, hi], rr.at[hi], x_send.at[5, i], x_recv.at[5, i], xm)

    def finish(i, lo, hi, both, ds):
        arrived(rl.at[hi], x_send.at[2, i], x_recv.at[2, i], xm)
        arrived(rr.at[lo], x_send.at[3, i], x_recv.at[3, i], xp)
        arrived(rl.at[lo], x_send.at[4, i], x_recv.at[4, i], xm)
        arrived(rr.at[hi], x_send.at[5, i], x_recv.at[5, i], xp)
        total = qf[both, :] + rl[both, :].astype(F32) + rr[both, :].astype(F32)
        qf[both] = total
        qb[both] = total.astype(BF16)
        for d in ds:
            send(qb.at[pl.ds((d + 8) % NZ * BAND, BAND)], rz.at[d], z_send.at[d], z_recv.at[d],
                 at(up_z(d), x, c))

    begin(0, far, far_lo, far_hi)
    begin(1, near, near_lo, near_hi)
    pair_landed(0)
    qf[...] = pair_sum(0, far + near)
    for d in (3, 9):
        arrived(p.at[c, x, from_z(d)], pz_send.at[d], pz_recv.at[d], zm)
    over = 3 - 6 * c
    band = p.at[c, x, lax.rem(z - over + NZ, NZ)]
    send(band, band, pz_send.at[6], pz_recv.at[6], at(lax.rem(z + over + NZ, NZ), x, c))
    for k in (2, 1):
        band_along(3, k)
        band_along(9, -k)
    middle(0, far_lo, far_hi)
    middle(1, near_lo, near_hi)
    finish(0, far_lo, far_hi, all_far, (6, 5, 7, 4, 8))
    finish(1, near_lo, near_hi, all_near, (3, 9, 2, 10, 1, 11))

    def bands(r, k=None):
        return p.at[c, up_x(r)] if k is None else p.at[c, up_x(r), pl.ds(k * (NZ // 2), NZ // 2)]

    def pass_bands(r, k, i, dev):
        send(bands(r, k), bands(r, k), px_send.at[i, k], px_recv.at[i, k], dev)

    def give_bands(r, i):
        send(bands(r), bands(r), pc_send.at[i], pc_recv.at[i], partner)

    for d in (1, 11, 2, 10, 4, 8, 5, 7, 6):
        arrived(p.at[c, x, from_z(d)], pz_send.at[d], pz_recv.at[d], zm)
    pass_bands(0, 0, 0, xp)
    pass_bands(0, 1, 1, xm)
    pass_bands(0, 1, 0, xp)
    pass_bands(0, 0, 1, xm)
    give_bands(0, 0)

    for d in NEAR:
        arrived(rz.at[d], z_send.at[d], z_recv.at[d], zm)
    total = qf[8 * BAND : 9 * BAND, :]
    for d in NEAR:
        total = total + rz[d].astype(F32)

    g[c, z, x] = total.astype(BF16)
    own_chunk = g.at[c, z, x]

    def bands_near():
        arrived(bands(3, 0), px_send.at[0, 0], px_recv.at[0, 0], xm)
        pass_bands(3, 0, 2, xp)
        arrived(bands(1, 1), px_send.at[1, 1], px_recv.at[1, 1], xp)
        pass_bands(1, 1, 2, xm)
        arrived(bands(3, 1), px_send.at[0, 1], px_recv.at[0, 1], xm)
        give_bands(3, 1)
        arrived(bands(1, 0), px_send.at[1, 0], px_recv.at[1, 0], xp)
        give_bands(1, 2)

    def bands_far():
        arrived(bands(2, 0), px_send.at[2, 0], px_recv.at[2, 0], xm)
        arrived(bands(2, 1), px_send.at[2, 1], px_recv.at[2, 1], xp)
        give_bands(2, 3)
        for i, r in ((0, 0), (1, 3), (2, 1), (3, 2)):
            arrived(p.at[1 - c, up_x(r)], pc_send.at[i], pc_recv.at[i], partner)

        def place(k, _):
            d = owner[k]
            cc, xx, zz = lax.rem(d, NC), lax.rem(d // NC, NX), d // (NC * NX)
            there = rows(k * BAND, BAND)
            pls[there, :] = p[cc, xx, zz, 0]
            prs[there, :] = p[cc, xx, zz, 1]
            return 0

        lax.fori_loop(0, NZ * NX * NC, place, 0, unroll=8)

    def z_then_x():
        def part(r, k=None):
            return g.at[c, :, up_x(r)] if k is None else g.at[c, pl.ds(k * (NZ // 2), NZ // 2), up_x(r)]

        def on(r, k, i, dev):
            send(part(r, k), part(r, k), gx_send.at[i, k], gx_recv.at[i, k], dev)

        def got(r, k, i):
            arrived(part(r, k), gx_send.at[i, k], gx_recv.at[i, k], xp)

        def give(r, i):
            send(part(r), part(r), gc_send.at[i], gc_recv.at[i], partner)

        for d in reversed(NEAR):
            send(own_chunk, own_chunk, gz_send.at[d], gz_recv.at[d], at(up_z(d), x, c))
        bands_near()
        for d in NEAR:
            arrived(g.at[c, from_z(d), x], gz_send.at[d], gz_recv.at[d], zm)
        on(0, 0, 0, xp)
        on(0, 1, 1, xm)
        on(0, 1, 0, xp)
        on(0, 0, 1, xm)
        give(0, 0)
        got(3, 0, 0)
        on(3, 0, 2, xp)
        got(1, 1, 1)
        on(1, 1, 2, xm)
        got(3, 1, 0)
        give(3, 1)
        got(1, 0, 1)
        give(1, 2)
        bands_far()
        got(2, 0, 2)
        got(2, 1, 2)
        give(2, 3)
        for d in [0] + NEAR:
            arrived(g.at[1 - c, from_z(d)], go_send.at[d], go_recv.at[d], partner)

    def x_then_z():
        def row(d):
            return g.at[c, from_z(d)]

        def on(d, k):
            to = (d + k) % NZ
            send(row(d), row(d), gz_send.at[to], gz_recv.at[to], at(up_z(k % NZ), x, c))

        def got(*ds):
            for d in ds:
                arrived(row(d), gz_send.at[d], gz_recv.at[d], zm)

        def give(*ds):
            for d in ds:
                send(row(d), row(d), go_send.at[d], go_recv.at[d], partner)

        for k in (2, 1, 3):
            send(own_chunk, own_chunk, gy_send.at[k], gy_recv.at[k], at(z, up_x(k), c))
        for k in (1, 3, 2):
            arrived(g.at[c, z, up_x(NX - k)], gy_send.at[k], gy_recv.at[k], xp)
        for k in (3, -3, 2, -2, 1, -1):
            on(0, k)
        give(0)
        bands_near()
        got(3, 9)
        six = g.at[c, up_z(3)]
        send(six, six, gz_send.at[6], gz_recv.at[6], at(up_z(NZ - 3), x, c))
        for k in (2, 1):
            on(3, k)
            on(9, -k)
        give(3, 9)
        got(1, 11, 2, 10)
        give(1, 11, 2, 10)
        bands_far()
        for d in (4, 8, 5, 7, 6):
            got(d)
            give(d)
        for i, r in ((0, 0), (1, 3), (2, 1), (3, 2)):
            arrived(g.at[1 - c, :, up_x(r)], gc_send.at[i], gc_recv.at[i], partner)

    started = list(pending)
    pending.clear()

    def finish_with(part):
        part()
        for made in pending:
            made.wait_send()
        pending.clear()

    @pl.when(c == 0)
    def _():
        finish_with(z_then_x)

    @pl.when(c == 1)
    def _():
        finish_with(x_then_z)

    pending.extend(started)
    for made in pending:
        made.wait_send()


def gather_all(owner, grad, left, right):
    vmem = pl.BlockSpec(memory_space=pltpu.VMEM)
    dma = pltpu.SemaphoreType.DMA
    return pl.pallas_call(
        exchange,
        out_shape=(
            jax.ShapeDtypeStruct((NC, NZ, NX, BAND, BLK), BF16),
            jax.ShapeDtypeStruct((ROWS, BLK), BF16),
            jax.ShapeDtypeStruct((ROWS, BLK), BF16),
        ),
        in_specs=[pl.BlockSpec(memory_space=pltpu.SMEM)] + [pl.BlockSpec(memory_space=pltpu.HBM)] * 3,
        out_specs=(vmem, vmem, vmem),
        scratch_shapes=[
            pltpu.VMEM((NC, NX, NZ, 2, BAND, BLK), BF16),
            pltpu.VMEM((NX, NZ, BAND, BLK), BF16),
            pltpu.VMEM((NX, NZ, BAND, BLK), BF16),
            pltpu.VMEM((NX, QUARTER, BLK), BF16),
            pltpu.VMEM((QUARTER, BLK), BF16),
            pltpu.VMEM((QUARTER, BLK), BF16),
            pltpu.VMEM((QUARTER, BLK), BF16),
            pltpu.VMEM((QUARTER, BLK), BF16),
            pltpu.VMEM((QUARTER, BLK), F32),
            pltpu.VMEM((QUARTER, BLK), BF16),
            pltpu.VMEM((NZ, BAND, BLK), BF16),
            pltpu.VMEM((QUARTER, BLK), F32),
            pltpu.VMEM((QUARTER, BLK), F32),
            dma((2 + NX,)),
            dma((NX,)), dma((NX,)),
            dma((6, 2)), dma((6, 2)),
            dma((NZ,)), dma((NZ,)),
            dma((NZ,)), dma((NZ,)),
            dma((3, 2)), dma((3, 2)),
            dma((NX,)), dma((NX,)),
            dma((NX,)), dma((NX,)),
            dma((NZ,)), dma((NZ,)),
            dma((3, 2)), dma((3, 2)),
            dma((NZ,)), dma((NZ,)),
            dma((NX,)), dma((NX,)),
        ],
        compiler_params=pltpu.CompilerParams(
            collective_id=0, has_side_effects=True, vmem_limit_bytes=40 << 20
        ),
    )(owner, grad, left, right)


def dots(owner, g, pls, prs, left_factor, right_factor, direction, left_out, right_out):
    me = lax.axis_index("dp")

    def find(k, own):
        return jnp.where(owner[k] == me, k, own)

    own = lax.fori_loop(0, NZ * NX * NC, find, jnp.int32(0), unroll=8)
    start = own * BAND
    block = start // BLK
    within = start - block * BLK
    row = g[pl.ds(pl.multiple_of(start, BAND), BAND), :]
    gb = g[pl.ds(pl.multiple_of(block * BLK, BLK), BLK), :]
    last = (((1,), (1,)), ((), ()))
    left_term = lax.dot_general(row, gb, last, preferred_element_type=F32)
    left_out[...] = BETA * left_factor[...] + (1.0 - BETA) * left_term
    which = lax.broadcasted_iota(jnp.int32, (BAND, BLK), 1)
    this = lax.broadcasted_iota(jnp.int32, (BAND, BLK), 0) + within
    onehot = jnp.where(which == this, 1.0, 0.0).astype(BF16)
    column = lax.dot_general(onehot, gb, last, preferred_element_type=F32).astype(BF16)
    right_term = jnp.dot(column, gb, preferred_element_type=F32)
    right_out[...] = BETA * right_factor[...] + (1.0 - BETA) * right_term
    for b in range(NB):
        at = pl.ds(b * BLK, BLK)
        mixed = jnp.dot(g[at, :], prs[at, :], preferred_element_type=F32).astype(BF16)
        direction[at, :] = jnp.dot(pls[at, :], mixed, preferred_element_type=F32).astype(BF16)


def precondition(owner, g, pls, prs, left_factor, right_factor):
    vmem = pl.BlockSpec(memory_space=pltpu.VMEM)
    return pl.pallas_call(
        dots,
        out_shape=(
            jax.ShapeDtypeStruct((ROWS, BLK), BF16),
            jax.ShapeDtypeStruct((BAND, BLK), F32),
            jax.ShapeDtypeStruct((BAND, BLK), F32),
        ),
        in_specs=[pl.BlockSpec(memory_space=pltpu.SMEM)] + [vmem] * 5,
        out_specs=(vmem, vmem, vmem),
        compiler_params=pltpu.CompilerParams(vmem_limit_bytes=40 << 20),
    )(owner, g, pls, prs, left_factor, right_factor)


def shards(partial_grads, band_owner, left_factor, right_factor, left_root, right_root):
    grad = partial_grads.reshape(NC, NZ, NX, BAND, BLK)
    held = [pltpu.with_memory_space_constraint(v, pltpu.HBM) for v in (band_owner, grad, left_root, right_root)]
    g, pls, prs = gather_all(*held)
    return precondition(band_owner, g.reshape(ROWS, BLK), pls, prs, left_factor, right_factor)


def solution(mesh):
    placed = (P("dp", None, "mp"), P(), P("dp", "mp"), P("dp", "mp"), P("dp", "mp"), P("dp", "mp"))
    return jax.shard_map(
        shards,
        mesh=mesh,
        in_specs=placed,
        out_specs=(P(None, "mp"), P("dp", "mp"), P("dp", "mp")),
        check_vma=False,
    )
```

```python
import functools

import jax
import jax.numpy as jnp
from jax import lax
from jax.experimental import pallas as pl
from jax.experimental.pallas import tpu as pltpu
from jax.sharding import PartitionSpec as P

BETA = 0.95
NZ, NX, NC = 12, 4, 2
BAND = 16
BLK = 512
NB = 3
ROWS = NB * BLK
HALF = ROWS // NC
QUARTER = HALF // NX
EIGHTH = QUARTER // 2
MESH = pl.DeviceIdType.MESH
F32 = jnp.float32
BF16 = jnp.bfloat16
NEAR = [1, 11, 2, 10, 3, 9, 4, 8, 5, 7, 6]


def exchange(
    owner, grad, left, right, g, pls, prs,
    p, half, r0, sb, ra, rb, rl, rr, qf, qb, rz, s1, s3,
    sem_local, c_send, c_recv, x_send, x_recv, z_send, z_recv,
    gz_send, gz_recv, gy_send, gy_recv, gc_send, gc_recv, go_send, go_recv,
    px_send, px_recv, pz_send, pz_recv, pc_send, pc_recv,
):
    me = lax.axis_index("dp")
    c = lax.rem(me, NC)
    x = lax.rem(me // NC, NX)
    z = me // (NC * NX)

    def at(zz, xx, cc):
        return (zz * NX + xx) * NC + cc

    def up_x(k):
        return lax.rem(x + k, NX)

    def up_z(k):
        return lax.rem(z + k, NZ)

    partner = at(z, x, 1 - c)
    xp, xm = at(z, up_x(1), c), at(z, up_x(3), c)
    zp, zm = at(up_z(1), x, c), at(up_z(NZ - 1), x, c)
    pending = []

    def copy(src, dst, ss, rs, dev):
        return pltpu.make_async_remote_copy(
            src_ref=src, dst_ref=dst, send_sem=ss, recv_sem=rs,
            device_id={"dp": dev}, device_id_type=MESH,
        )

    def send(*args):
        made = copy(*args)
        made.start()
        pending.append(made)

    def arrived(dst, ss, rs, dev):
        copy(dst, dst, ss, rs, dev).wait_recv()

    barrier = pltpu.get_barrier_semaphore()
    others = [at(up_z(k), x, c) for k in reversed(NEAR)]
    others += [at(z, up_x(k), c) for k in (2, 1, 3)] + [partner]
    for dev in others:
        pl.semaphore_signal(barrier, inc=1, device_id={"dp": dev}, device_id_type=MESH)

    def rows(start, size):
        return pl.ds(pl.multiple_of(start, BAND), size)

    slot = p.at[c, x, z]
    own = [
        pltpu.make_async_copy(left, slot.at[0], sem_local.at[0]),
        pltpu.make_async_copy(right, slot.at[1], sem_local.at[1]),
    ]
    loads = {
        r: pltpu.make_async_copy(
            grad.at[c, :, up_x(r)], half.at[r], sem_local.at[2 + r]
        )
        for r in (2, 1, 3, 0)
    }
    for one in own + list(loads.values()):
        one.start()
    pl.semaphore_wait(barrier, len(others))

    for r in (2, 1, 3, 0):
        send(
            grad.at[1 - c, :, up_x(r)],
            r0.at[r], c_send.at[r], c_recv.at[r], partner,
        )
    for one in own:
        one.wait()
    def from_z(d):
        return up_z(NZ - d)

    def band_along(d, k):
        band = p.at[c, x, from_z(d)]
        to = (d + k) % NZ
        send(band, band, pz_send.at[to], pz_recv.at[to], at(up_z(k % NZ), x, c))

    for k in (3, -3, 2, -2, 1, -1):
        band_along(0, k)

    far = list(range(4, 9))
    near = list(range(9, 12)) + list(range(0, 4))
    far_lo, far_hi = pl.ds(0, 3 * BAND), pl.ds(3 * BAND, 2 * BAND)
    near_lo, near_hi = pl.ds(5 * BAND, 4 * BAND), pl.ds(9 * BAND, 3 * BAND)
    all_far, all_near = pl.ds(0, 5 * BAND), pl.ds(5 * BAND, 7 * BAND)

    def pair_landed(r):
        loads[r].wait()
        arrived(r0.at[r], c_send.at[r], c_recv.at[r], partner)

    def pair_sum(r, ds):
        return jnp.concatenate(
            [half[r, up_z(d)].astype(F32) + r0[r, up_z(d)].astype(F32) for d in ds],
            axis=0,
        )

    def begin(i, ds, lo, hi):
        if i == 0:
            pair_landed(2)
        total = pair_sum(2, ds).astype(BF16)
        cut = lo.size
        sb[2, lo], sb[2, hi] = total[:cut], total[cut:]
        send(sb.at[2, lo], ra.at[lo], x_send.at[0, i], x_recv.at[0, i], xp)
        send(sb.at[2, hi], rb.at[hi], x_send.at[1, i], x_recv.at[1, i], xm)
        if i == 0:
            pair_landed(1)
        total = pair_sum(1, ds)
        s1[lo] = total[:cut]
        sb[1, hi] = total[cut:].astype(BF16)
        send(sb.at[1, hi], rl.at[hi], x_send.at[2, i], x_recv.at[2, i], xp)
        if i == 0:
            pair_landed(3)
        total = pair_sum(3, ds)
        s3[hi] = total[cut:]
        sb[3, lo] = total[:cut].astype(BF16)
        send(sb.at[3, lo], rr.at[lo], x_send.at[3, i], x_recv.at[3, i], xm)

    def middle(i, lo, hi):
        arrived(ra.at[lo], x_send.at[0, i], x_recv.at[0, i], xm)
        sb[1, lo] = (s1[lo, :] + ra[lo, :].astype(F32)).astype(BF16)
        send(sb.at[1, lo], rl.at[lo], x_send.at[4, i], x_recv.at[4, i], xp)
        arrived(rb.at[hi], x_send.at[1, i], x_recv.at[1, i], xp)
        sb[3, hi] = (s3[hi, :] + rb[hi, :].astype(F32)).astype(BF16)
        send(sb.at[3, hi], rr.at[hi], x_send.at[5, i], x_recv.at[5, i], xm)

    def finish(i, lo, hi, both, ds):
        arrived(rl.at[hi], x_send.at[2, i], x_recv.at[2, i], xm)
        arrived(rr.at[lo], x_send.at[3, i], x_recv.at[3, i], xp)
        arrived(rl.at[lo], x_send.at[4, i], x_recv.at[4, i], xm)
        arrived(rr.at[hi], x_send.at[5, i], x_recv.at[5, i], xp)
        total = qf[both, :] + rl[both, :].astype(F32) + rr[both, :].astype(F32)
        qf[both] = total
        qb[both] = total.astype(BF16)
        for d in ds:
            send(qb.at[pl.ds((d + 8) % NZ * BAND, BAND)], rz.at[d], z_send.at[d], z_recv.at[d],
                 at(up_z(d), x, c))

    begin(0, far, far_lo, far_hi)
    begin(1, near, near_lo, near_hi)
    pair_landed(0)
    qf[...] = pair_sum(0, far + near)
    for d in (3, 9):
        arrived(p.at[c, x, from_z(d)], pz_send.at[d], pz_recv.at[d], zm)
    over = 3 - 6 * c
    band = p.at[c, x, lax.rem(z - over + NZ, NZ)]
    send(band, band, pz_send.at[6], pz_recv.at[6], at(lax.rem(z + over + NZ, NZ), x, c))
    for k in (2, 1):
        band_along(3, k)
        band_along(9, -k)
    middle(0, far_lo, far_hi)
    middle(1, near_lo, near_hi)
    finish(0, far_lo, far_hi, all_far, (6, 5, 7, 4, 8))
    finish(1, near_lo, near_hi, all_near, (3, 9, 2, 10, 1, 11))

    def bands(r, k=None):
        return p.at[c, up_x(r)] if k is None else p.at[c, up_x(r), pl.ds(k * (NZ // 2), NZ // 2)]

    def pass_bands(r, k, i, dev):
        send(bands(r, k), bands(r, k), px_send.at[i, k], px_recv.at[i, k], dev)

    def give_bands(r, i):
        send(bands(r), bands(r), pc_send.at[i], pc_recv.at[i], partner)

    for d in (1, 11, 2, 10, 4, 8, 5, 7, 6):
        arrived(p.at[c, x, from_z(d)], pz_send.at[d], pz_recv.at[d], zm)
    pass_bands(0, 0, 0, xp)
    pass_bands(0, 1, 1, xm)
    pass_bands(0, 1, 0, xp)
    pass_bands(0, 0, 1, xm)
    give_bands(0, 0)

    for d in NEAR:
        arrived(rz.at[d], z_send.at[d], z_recv.at[d], zm)
    total = qf[8 * BAND : 9 * BAND, :]
    for d in NEAR:
        total = total + rz[d].astype(F32)

    g[c, z, x] = total.astype(BF16)
    own_chunk = g.at[c, z, x]

    def bands_near():
        arrived(bands(3, 0), px_send.at[0, 0], px_recv.at[0, 0], xm)
        pass_bands(3, 0, 2, xp)
        arrived(bands(1, 1), px_send.at[1, 1], px_recv.at[1, 1], xp)
        pass_bands(1, 1, 2, xm)
        arrived(bands(3, 1), px_send.at[0, 1], px_recv.at[0, 1], xm)
        give_bands(3, 1)
        arrived(bands(1, 0), px_send.at[1, 0], px_recv.at[1, 0], xp)
        give_bands(1, 2)

    def bands_far():
        arrived(bands(2, 0), px_send.at[2, 0], px_recv.at[2, 0], xm)
        arrived(bands(2, 1), px_send.at[2, 1], px_recv.at[2, 1], xp)
        give_bands(2, 3)

    def bands_in_order():
        for i, r in ((0, 0), (1, 3), (2, 1), (3, 2)):
            arrived(p.at[1 - c, up_x(r)], pc_send.at[i], pc_recv.at[i], partner)

        def place(k, _):
            d = owner[k]
            cc, xx, zz = lax.rem(d, NC), lax.rem(d // NC, NX), d // (NC * NX)
            there = rows(k * BAND, BAND)
            pls[there, :] = p[cc, xx, zz, 0]
            prs[there, :] = p[cc, xx, zz, 1]
            return 0

        lax.fori_loop(0, NZ * NX * NC, place, 0, unroll=8)

    def z_then_x():
        def part(r, k=None):
            return g.at[c, :, up_x(r)] if k is None else g.at[c, pl.ds(k * (NZ // 2), NZ // 2), up_x(r)]

        def give(r, i):
            send(part(r), part(r), gc_send.at[i], gc_recv.at[i], partner)

        for d in reversed(NEAR):
            send(own_chunk, own_chunk, gz_send.at[d], gz_recv.at[d], at(up_z(d), x, c))
        bands_near()
        for d in NEAR:
            arrived(g.at[c, from_z(d), x], gz_send.at[d], gz_recv.at[d], zm)
        for k in (2, 1, 3):
            send(part(0), part(0), gy_send.at[k], gy_recv.at[k], at(z, up_x(k), c))
        give(0, 0)
        bands_far()
        for k, i in ((1, 1), (3, 2), (2, 3)):
            arrived(part(NX - k), gy_send.at[k], gy_recv.at[k], xp)
            give(NX - k, i)
        bands_in_order()
        for d in [0] + NEAR:
            arrived(g.at[1 - c, from_z(d)], go_send.at[d], go_recv.at[d], partner)

    def x_then_z():
        def row(d):
            return g.at[c, from_z(d)]

        def on(d, k):
            to = (d + k) % NZ
            send(row(d), row(d), gz_send.at[to], gz_recv.at[to], at(up_z(k % NZ), x, c))

        def got(*ds):
            for d in ds:
                arrived(row(d), gz_send.at[d], gz_recv.at[d], zm)

        def give(*ds):
            for d in ds:
                send(row(d), row(d), go_send.at[d], go_recv.at[d], partner)

        for k in (2, 1, 3):
            send(own_chunk, own_chunk, gy_send.at[k], gy_recv.at[k], at(z, up_x(k), c))
        for k in (1, 3, 2):
            arrived(g.at[c, z, up_x(NX - k)], gy_send.at[k], gy_recv.at[k], xp)
        for k in (3, -3, 2, -2, 1, -1):
            on(0, k)
        give(0)
        bands_near()
        got(3, 9)
        six = g.at[c, up_z(3)]
        send(six, six, gz_send.at[6], gz_recv.at[6], at(up_z(NZ - 3), x, c))
        for k in (2, 1):
            on(3, k)
            on(9, -k)
        give(3, 9)
        got(1, 11, 2, 10)
        give(1, 11, 2, 10)
        bands_far()
        for d in (4, 8, 5, 7, 6):
            got(d)
            give(d)
        bands_in_order()
        for i, r in ((0, 0), (1, 3), (2, 1), (3, 2)):
            arrived(g.at[1 - c, :, up_x(r)], gc_send.at[i], gc_recv.at[i], partner)

    started = list(pending)
    pending.clear()

    def finish_with(part):
        part()
        for made in pending:
            made.wait_send()
        pending.clear()

    @pl.when(c == 0)
    def _():
        finish_with(z_then_x)

    @pl.when(c == 1)
    def _():
        finish_with(x_then_z)

    pending.extend(started)
    for made in pending:
        made.wait_send()


def gather_all(owner, grad, left, right):
    vmem = pl.BlockSpec(memory_space=pltpu.VMEM)
    dma = pltpu.SemaphoreType.DMA
    return pl.pallas_call(
        exchange,
        out_shape=(
            jax.ShapeDtypeStruct((NC, NZ, NX, BAND, BLK), BF16),
            jax.ShapeDtypeStruct((ROWS, BLK), BF16),
            jax.ShapeDtypeStruct((ROWS, BLK), BF16),
        ),
        in_specs=[pl.BlockSpec(memory_space=pltpu.SMEM)] + [pl.BlockSpec(memory_space=pltpu.HBM)] * 3,
        out_specs=(vmem, vmem, vmem),
        scratch_shapes=[
            pltpu.VMEM((NC, NX, NZ, 2, BAND, BLK), BF16),
            pltpu.VMEM((NX, NZ, BAND, BLK), BF16),
            pltpu.VMEM((NX, NZ, BAND, BLK), BF16),
            pltpu.VMEM((NX, QUARTER, BLK), BF16),
            pltpu.VMEM((QUARTER, BLK), BF16),
            pltpu.VMEM((QUARTER, BLK), BF16),
            pltpu.VMEM((QUARTER, BLK), BF16),
            pltpu.VMEM((QUARTER, BLK), BF16),
            pltpu.VMEM((QUARTER, BLK), F32),
            pltpu.VMEM((QUARTER, BLK), BF16),
            pltpu.VMEM((NZ, BAND, BLK), BF16),
            pltpu.VMEM((QUARTER, BLK), F32),
            pltpu.VMEM((QUARTER, BLK), F32),
            dma((2 + NX,)),
            dma((NX,)), dma((NX,)),
            dma((6, 2)), dma((6, 2)),
            dma((NZ,)), dma((NZ,)),
            dma((NZ,)), dma((NZ,)),
            dma((NX,)), dma((NX,)),
            dma((NX,)), dma((NX,)),
            dma((NZ,)), dma((NZ,)),
            dma((3, 2)), dma((3, 2)),
            dma((NZ,)), dma((NZ,)),
            dma((NX,)), dma((NX,)),
        ],
        compiler_params=pltpu.CompilerParams(
            collective_id=0, has_side_effects=True, vmem_limit_bytes=40 << 20
        ),
    )(owner, grad, left, right)


def dots(owner, g, pls, prs, left_factor, right_factor, direction, left_out, right_out):
    me = lax.axis_index("dp")

    def find(k, own):
        return jnp.where(owner[k] == me, k, own)

    own = lax.fori_loop(0, NZ * NX * NC, find, jnp.int32(0), unroll=8)
    start = own * BAND
    block = start // BLK
    within = start - block * BLK
    row = g[pl.ds(pl.multiple_of(start, BAND), BAND), :]
    gb = g[pl.ds(pl.multiple_of(block * BLK, BLK), BLK), :]
    last = (((1,), (1,)), ((), ()))
    left_term = lax.dot_general(row, gb, last, preferred_element_type=F32)
    left_out[...] = BETA * left_factor[...] + (1.0 - BETA) * left_term
    which = lax.broadcasted_iota(jnp.int32, (BAND, BLK), 1)
    this = lax.broadcasted_iota(jnp.int32, (BAND, BLK), 0) + within
    onehot = jnp.where(which == this, 1.0, 0.0).astype(BF16)
    column = lax.dot_general(onehot, gb, last, preferred_element_type=F32).astype(BF16)
    right_term = jnp.dot(column, gb, preferred_element_type=F32)
    right_out[...] = BETA * right_factor[...] + (1.0 - BETA) * right_term
    for b in range(NB):
        at = pl.ds(b * BLK, BLK)
        mixed = jnp.dot(g[at, :], prs[at, :], preferred_element_type=F32).astype(BF16)
        direction[at, :] = jnp.dot(pls[at, :], mixed, preferred_element_type=F32).astype(BF16)


def precondition(owner, g, pls, prs, left_factor, right_factor):
    vmem = pl.BlockSpec(memory_space=pltpu.VMEM)
    return pl.pallas_call(
        dots,
        out_shape=(
            jax.ShapeDtypeStruct((ROWS, BLK), BF16),
            jax.ShapeDtypeStruct((BAND, BLK), F32),
            jax.ShapeDtypeStruct((BAND, BLK), F32),
        ),
        in_specs=[pl.BlockSpec(memory_space=pltpu.SMEM)] + [vmem] * 5,
        out_specs=(vmem, vmem, vmem),
        compiler_params=pltpu.CompilerParams(vmem_limit_bytes=40 << 20),
    )(owner, g, pls, prs, left_factor, right_factor)


def shards(partial_grads, band_owner, left_factor, right_factor, left_root, right_root):
    grad = partial_grads.reshape(NC, NZ, NX, BAND, BLK)
    held = [pltpu.with_memory_space_constraint(v, pltpu.HBM) for v in (band_owner, grad, left_root, right_root)]
    g, pls, prs = gather_all(*held)
    return precondition(band_owner, g.reshape(ROWS, BLK), pls, prs, left_factor, right_factor)


def solution(mesh):
    placed = (P("dp", None, "mp"), P(), P("dp", "mp"), P("dp", "mp"), P("dp", "mp"), P("dp", "mp"))
    return jax.shard_map(
        shards,
        mesh=mesh,
        in_specs=placed,
        out_specs=(P(None, "mp"), P("dp", "mp"), P("dp", "mp")),
        check_vma=False,
    )
```

```python
import functools

import jax
import jax.numpy as jnp
from jax import lax
from jax.experimental import pallas as pl
from jax.experimental.pallas import tpu as pltpu
from jax.sharding import PartitionSpec as P

BETA = 0.95
NZ, NX, NC = 12, 4, 2
BAND = 16
BLK = 512
NB = 3
ROWS = NB * BLK
HALF = ROWS // NC
QUARTER = HALF // NX
EIGHTH = QUARTER // 2
MESH = pl.DeviceIdType.MESH
F32 = jnp.float32
BF16 = jnp.bfloat16
NEAR = [1, 11, 2, 10, 3, 9, 4, 8, 5, 7, 6]


def exchange(
    owner, grad, left, right, g, pls, prs,
    p, half, r0, sb, ra, rb, rl, rr, qf, qb, rz, s1, s3,
    sem_local, c_send, c_recv, x_send, x_recv, z_send, z_recv,
    gz_send, gz_recv, gy_send, gy_recv, gc_send, gc_recv, go_send, go_recv,
    px_send, px_recv, pz_send, pz_recv, pc_send, pc_recv,
):
    me = lax.axis_index("dp")
    c = lax.rem(me, NC)
    x = lax.rem(me // NC, NX)
    z = me // (NC * NX)

    def at(zz, xx, cc):
        return (zz * NX + xx) * NC + cc

    def up_x(k):
        return lax.rem(x + k, NX)

    def up_z(k):
        return lax.rem(z + k, NZ)

    partner = at(z, x, 1 - c)
    xp, xm = at(z, up_x(1), c), at(z, up_x(3), c)
    zp, zm = at(up_z(1), x, c), at(up_z(NZ - 1), x, c)
    pending = []

    def copy(src, dst, ss, rs, dev):
        return pltpu.make_async_remote_copy(
            src_ref=src, dst_ref=dst, send_sem=ss, recv_sem=rs,
            device_id={"dp": dev}, device_id_type=MESH,
        )

    def send(*args):
        made = copy(*args)
        made.start()
        pending.append(made)

    def arrived(dst, ss, rs, dev):
        copy(dst, dst, ss, rs, dev).wait_recv()

    barrier = pltpu.get_barrier_semaphore()
    others = [at(up_z(k), x, c) for k in reversed(NEAR)]
    others += [at(z, up_x(k), c) for k in (2, 1, 3)] + [partner]
    for dev in others:
        pl.semaphore_signal(barrier, inc=1, device_id={"dp": dev}, device_id_type=MESH)

    def rows(start, size):
        return pl.ds(pl.multiple_of(start, BAND), size)

    slot = p.at[c, x, z]
    own = [
        pltpu.make_async_copy(left, slot.at[0], sem_local.at[0]),
        pltpu.make_async_copy(right, slot.at[1], sem_local.at[1]),
    ]
    loads = {
        r: pltpu.make_async_copy(
            grad.at[c, :, up_x(r)], half.at[r], sem_local.at[2 + r]
        )
        for r in (2, 1, 3, 0)
    }
    for one in own + list(loads.values()):
        one.start()
    pl.semaphore_wait(barrier, len(others))

    for r in (2, 1, 3, 0):
        send(
            grad.at[1 - c, :, up_x(r)],
            r0.at[r], c_send.at[r], c_recv.at[r], partner,
        )
    for one in own:
        one.wait()
    def from_z(d):
        return up_z(NZ - d)

    def band_along(d, k):
        band = p.at[c, x, from_z(d)]
        to = (d + k) % NZ
        send(band, band, pz_send.at[to], pz_recv.at[to], at(up_z(k % NZ), x, c))

    for k in (3, -3, 2, -2, 1, -1):
        band_along(0, k)

    far = list(range(4, 9))
    near = list(range(9, 12)) + list(range(0, 4))
    far_lo, far_hi = pl.ds(0, 3 * BAND), pl.ds(3 * BAND, 2 * BAND)
    near_lo, near_hi = pl.ds(5 * BAND, 4 * BAND), pl.ds(9 * BAND, 3 * BAND)
    all_far, all_near = pl.ds(0, 5 * BAND), pl.ds(5 * BAND, 7 * BAND)

    def pair_landed(r):
        loads[r].wait()
        arrived(r0.at[r], c_send.at[r], c_recv.at[r], partner)

    def pair_sum(r, ds):
        return jnp.concatenate(
            [half[r, up_z(d)].astype(F32) + r0[r, up_z(d)].astype(F32) for d in ds],
            axis=0,
        )

    def begin(i, ds, lo, hi):
        if i == 0:
            pair_landed(2)
        total = pair_sum(2, ds).astype(BF16)
        cut = lo.size
        sb[2, lo], sb[2, hi] = total[:cut], total[cut:]
        send(sb.at[2, lo], ra.at[lo], x_send.at[0, i], x_recv.at[0, i], xp)
        send(sb.at[2, hi], rb.at[hi], x_send.at[1, i], x_recv.at[1, i], xm)
        if i == 0:
            pair_landed(1)
        total = pair_sum(1, ds)
        s1[lo] = total[:cut]
        sb[1, hi] = total[cut:].astype(BF16)
        send(sb.at[1, hi], rl.at[hi], x_send.at[2, i], x_recv.at[2, i], xp)
        if i == 0:
            pair_landed(3)
        total = pair_sum(3, ds)
        s3[hi] = total[cut:]
        sb[3, lo] = total[:cut].astype(BF16)
        send(sb.at[3, lo], rr.at[lo], x_send.at[3, i], x_recv.at[3, i], xm)

    def middle(i, lo, hi):
        arrived(ra.at[lo], x_send.at[0, i], x_recv.at[0, i], xm)
        sb[1, lo] = (s1[lo, :] + ra[lo, :].astype(F32)).astype(BF16)
        send(sb.at[1, lo], rl.at[lo], x_send.at[4, i], x_recv.at[4, i], xp)
        arrived(rb.at[hi], x_send.at[1, i], x_recv.at[1, i], xp)
        sb[3, hi] = (s3[hi, :] + rb[hi, :].astype(F32)).astype(BF16)
        send(sb.at[3, hi], rr.at[hi], x_send.at[5, i], x_recv.at[5, i], xm)

    def finish(i, lo, hi, both, ds):
        arrived(rl.at[hi], x_send.at[2, i], x_recv.at[2, i], xm)
        arrived(rr.at[lo], x_send.at[3, i], x_recv.at[3, i], xp)
        arrived(rl.at[lo], x_send.at[4, i], x_recv.at[4, i], xm)
        arrived(rr.at[hi], x_send.at[5, i], x_recv.at[5, i], xp)
        total = qf[both, :] + rl[both, :].astype(F32) + rr[both, :].astype(F32)
        qf[both] = total
        qb[both] = total.astype(BF16)
        for d in ds:
            send(qb.at[pl.ds((d + 8) % NZ * BAND, BAND)], rz.at[d], z_send.at[d], z_recv.at[d],
                 at(up_z(d), x, c))

    begin(0, far, far_lo, far_hi)
    begin(1, near, near_lo, near_hi)
    pair_landed(0)
    qf[...] = pair_sum(0, far + near)
    for d in (3, 9):
        arrived(p.at[c, x, from_z(d)], pz_send.at[d], pz_recv.at[d], zm)
    over = 3 - 6 * c
    band = p.at[c, x, lax.rem(z - over + NZ, NZ)]
    send(band, band, pz_send.at[6], pz_recv.at[6], at(lax.rem(z + over + NZ, NZ), x, c))
    for k in (2, 1):
        band_along(3, k)
        band_along(9, -k)
    middle(0, far_lo, far_hi)
    middle(1, near_lo, near_hi)
    finish(0, far_lo, far_hi, all_far, (6, 5, 7, 4, 8))
    finish(1, near_lo, near_hi, all_near, (3, 9, 2, 10, 1, 11))

    def bands(r, k=None):
        return p.at[c, up_x(r)] if k is None else p.at[c, up_x(r), pl.ds(k * (NZ // 2), NZ // 2)]

    def pass_bands(r, k, i, dev):
        send(bands(r, k), bands(r, k), px_send.at[i, k], px_recv.at[i, k], dev)

    def give_bands(r, i):
        send(bands(r), bands(r), pc_send.at[i], pc_recv.at[i], partner)

    for d in (1, 11, 2, 10, 4, 8, 5, 7, 6):
        arrived(p.at[c, x, from_z(d)], pz_send.at[d], pz_recv.at[d], zm)
    pass_bands(0, 0, 0, xp)
    pass_bands(0, 1, 1, xm)
    pass_bands(0, 1, 0, xp)
    pass_bands(0, 0, 1, xm)
    give_bands(0, 0)

    for d in NEAR:
        arrived(rz.at[d], z_send.at[d], z_recv.at[d], zm)
    total = qf[8 * BAND : 9 * BAND, :]
    for d in NEAR:
        total = total + rz[d].astype(F32)

    g[c, z, x] = total.astype(BF16)
    own_chunk = g.at[c, z, x]

    def bands_near():
        arrived(bands(3, 0), px_send.at[0, 0], px_recv.at[0, 0], xm)
        pass_bands(3, 0, 2, xp)
        arrived(bands(1, 1), px_send.at[1, 1], px_recv.at[1, 1], xp)
        pass_bands(1, 1, 2, xm)
        arrived(bands(3, 1), px_send.at[0, 1], px_recv.at[0, 1], xm)
        give_bands(3, 1)
        arrived(bands(1, 0), px_send.at[1, 0], px_recv.at[1, 0], xp)
        give_bands(1, 2)

    def bands_far():
        arrived(bands(2, 0), px_send.at[2, 0], px_recv.at[2, 0], xm)
        arrived(bands(2, 1), px_send.at[2, 1], px_recv.at[2, 1], xp)
        give_bands(2, 3)

    def bands_in_order():
        for i, r in ((0, 0), (1, 3), (2, 1), (3, 2)):
            arrived(p.at[1 - c, up_x(r)], pc_send.at[i], pc_recv.at[i], partner)

        def place(k, _):
            d = owner[k]
            cc, xx, zz = lax.rem(d, NC), lax.rem(d // NC, NX), d // (NC * NX)
            there = rows(k * BAND, BAND)
            pls[there, :] = p[cc, xx, zz, 0]
            prs[there, :] = p[cc, xx, zz, 1]
            return 0

        lax.fori_loop(0, NZ * NX * NC, place, 0, unroll=8)

    def z_then_x():
        def part(r, k=None):
            return g.at[c, :, up_x(r)] if k is None else g.at[c, pl.ds(k * (NZ // 2), NZ // 2), up_x(r)]

        def give(r, i):
            send(part(r), part(r), gc_send.at[i], gc_recv.at[i], partner)

        for d in reversed(NEAR):
            send(own_chunk, own_chunk, gz_send.at[d], gz_recv.at[d], at(up_z(d), x, c))
        bands_near()
        six = NZ // 2
        base = z // six * six
        other = six - base

        def half_of(r, start):
            return g.at[c, pl.ds(start, six), up_x(r)]

        def got_z(zz):
            d = lax.rem(z - zz + NZ, NZ)
            arrived(g.at[c, zz, x], gz_send.at[d], gz_recv.at[d], zm)

        def on(h, start):
            for k in (2, 1, 3):
                send(half_of(0, start), half_of(0, start),
                     gy_send.at[h, k], gy_recv.at[h, k], at(z, up_x(k), c))

        for k in (1, 5, 2, 4, 3):
            got_z(base + lax.rem(z - base + k, six))
        on(0, base)
        for k in range(six):
            got_z(other + k)
        on(1, other)
        give(0, 0)
        bands_far()
        for k, i in ((1, 1), (3, 2), (2, 3)):
            arrived(half_of(NX - k, base), gy_send.at[0, k], gy_recv.at[0, k], xp)
            arrived(half_of(NX - k, other), gy_send.at[1, k], gy_recv.at[1, k], xp)
            give(NX - k, i)
        bands_in_order()
        for d in [0] + NEAR:
            arrived(g.at[1 - c, from_z(d)], go_send.at[d], go_recv.at[d], partner)

    def x_then_z():
        def row(d):
            return g.at[c, from_z(d)]

        def on(d, k):
            to = (d + k) % NZ
            send(row(d), row(d), gz_send.at[to], gz_recv.at[to], at(up_z(k % NZ), x, c))

        def got(*ds):
            for d in ds:
                arrived(row(d), gz_send.at[d], gz_recv.at[d], zm)

        def give(*ds):
            for d in ds:
                send(row(d), row(d), go_send.at[d], go_recv.at[d], partner)

        for k in (2, 1, 3):
            send(own_chunk, own_chunk, gy_send.at[0, k], gy_recv.at[0, k], at(z, up_x(k), c))
        for k in (1, 3, 2):
            arrived(g.at[c, z, up_x(NX - k)], gy_send.at[0, k], gy_recv.at[0, k], xp)
        for k in (3, -3, 2, -2, 1, -1):
            on(0, k)
        give(0)
        bands_near()
        got(3, 9)
        six = g.at[c, up_z(3)]
        send(six, six, gz_send.at[6], gz_recv.at[6], at(up_z(NZ - 3), x, c))
        for k in (2, 1):
            on(3, k)
            on(9, -k)
        give(3, 9)
        got(1, 11, 2, 10)
        give(1, 11, 2, 10)
        bands_far()
        for d in (4, 8, 5, 7, 6):
            got(d)
            give(d)
        bands_in_order()
        for i, r in ((0, 0), (1, 3), (2, 1), (3, 2)):
            arrived(g.at[1 - c, :, up_x(r)], gc_send.at[i], gc_recv.at[i], partner)

    started = list(pending)
    pending.clear()

    def finish_with(part):
        part()
        for made in pending:
            made.wait_send()
        pending.clear()

    @pl.when(c == 0)
    def _():
        finish_with(z_then_x)

    @pl.when(c == 1)
    def _():
        finish_with(x_then_z)

    pending.extend(started)
    for made in pending:
        made.wait_send()


def gather_all(owner, grad, left, right):
    vmem = pl.BlockSpec(memory_space=pltpu.VMEM)
    dma = pltpu.SemaphoreType.DMA
    return pl.pallas_call(
        exchange,
        out_shape=(
            jax.ShapeDtypeStruct((NC, NZ, NX, BAND, BLK), BF16),
            jax.ShapeDtypeStruct((ROWS, BLK), BF16),
            jax.ShapeDtypeStruct((ROWS, BLK), BF16),
        ),
        in_specs=[pl.BlockSpec(memory_space=pltpu.SMEM)] + [pl.BlockSpec(memory_space=pltpu.HBM)] * 3,
        out_specs=(vmem, vmem, vmem),
        scratch_shapes=[
            pltpu.VMEM((NC, NX, NZ, 2, BAND, BLK), BF16),
            pltpu.VMEM((NX, NZ, BAND, BLK), BF16),
            pltpu.VMEM((NX, NZ, BAND, BLK), BF16),
            pltpu.VMEM((NX, QUARTER, BLK), BF16),
            pltpu.VMEM((QUARTER, BLK), BF16),
            pltpu.VMEM((QUARTER, BLK), BF16),
            pltpu.VMEM((QUARTER, BLK), BF16),
            pltpu.VMEM((QUARTER, BLK), BF16),
            pltpu.VMEM((QUARTER, BLK), F32),
            pltpu.VMEM((QUARTER, BLK), BF16),
            pltpu.VMEM((NZ, BAND, BLK), BF16),
            pltpu.VMEM((QUARTER, BLK), F32),
            pltpu.VMEM((QUARTER, BLK), F32),
            dma((2 + NX,)),
            dma((NX,)), dma((NX,)),
            dma((6, 2)), dma((6, 2)),
            dma((NZ,)), dma((NZ,)),
            dma((NZ,)), dma((NZ,)),
            dma((2, NX)), dma((2, NX)),
            dma((NX,)), dma((NX,)),
            dma((NZ,)), dma((NZ,)),
            dma((3, 2)), dma((3, 2)),
            dma((NZ,)), dma((NZ,)),
            dma((NX,)), dma((NX,)),
        ],
        compiler_params=pltpu.CompilerParams(
            collective_id=0, has_side_effects=True, vmem_limit_bytes=40 << 20
        ),
    )(owner, grad, left, right)


def dots(owner, g, pls, prs, left_factor, right_factor, direction, left_out, right_out):
    me = lax.axis_index("dp")

    def find(k, own):
        return jnp.where(owner[k] == me, k, own)

    own = lax.fori_loop(0, NZ * NX * NC, find, jnp.int32(0), unroll=8)
    start = own * BAND
    block = start // BLK
    within = start - block * BLK
    row = g[pl.ds(pl.multiple_of(start, BAND), BAND), :]
    gb = g[pl.ds(pl.multiple_of(block * BLK, BLK), BLK), :]
    last = (((1,), (1,)), ((), ()))
    left_term = lax.dot_general(row, gb, last, preferred_element_type=F32)
    left_out[...] = BETA * left_factor[...] + (1.0 - BETA) * left_term
    which = lax.broadcasted_iota(jnp.int32, (BAND, BLK), 1)
    this = lax.broadcasted_iota(jnp.int32, (BAND, BLK), 0) + within
    onehot = jnp.where(which == this, 1.0, 0.0).astype(BF16)
    column = lax.dot_general(onehot, gb, last, preferred_element_type=F32).astype(BF16)
    right_term = jnp.dot(column, gb, preferred_element_type=F32)
    right_out[...] = BETA * right_factor[...] + (1.0 - BETA) * right_term
    def mix(b):
        at = pl.ds(b * BLK, BLK)
        return jnp.dot(g[at, :], prs[at, :], preferred_element_type=F32).astype(BF16)

    def direct(b, mixed):
        at = pl.ds(b * BLK, BLK)
        direction[at, :] = jnp.dot(pls[at, :], mixed, preferred_element_type=F32).astype(BF16)

    mixed = mix(0)
    for b in range(1, NB):
        later = mix(b)
        direct(b - 1, mixed)
        mixed = later
    direct(NB - 1, mixed)


def precondition(owner, g, pls, prs, left_factor, right_factor):
    vmem = pl.BlockSpec(memory_space=pltpu.VMEM)
    return pl.pallas_call(
        dots,
        out_shape=(
            jax.ShapeDtypeStruct((ROWS, BLK), BF16),
            jax.ShapeDtypeStruct((BAND, BLK), F32),
            jax.ShapeDtypeStruct((BAND, BLK), F32),
        ),
        in_specs=[pl.BlockSpec(memory_space=pltpu.SMEM)] + [vmem] * 5,
        out_specs=(vmem, vmem, vmem),
        compiler_params=pltpu.CompilerParams(vmem_limit_bytes=40 << 20),
    )(owner, g, pls, prs, left_factor, right_factor)


def shards(partial_grads, band_owner, left_factor, right_factor, left_root, right_root):
    grad = partial_grads.reshape(NC, NZ, NX, BAND, BLK)
    held = [pltpu.with_memory_space_constraint(v, pltpu.HBM) for v in (band_owner, grad, left_root, right_root)]
    g, pls, prs = gather_all(*held)
    return precondition(band_owner, g.reshape(ROWS, BLK), pls, prs, left_factor, right_factor)


def solution(mesh):
    placed = (P("dp", None, "mp"), P(), P("dp", "mp"), P("dp", "mp"), P("dp", "mp"), P("dp", "mp"))
    return jax.shard_map(
        shards,
        mesh=mesh,
        in_specs=placed,
        out_specs=(P(None, "mp"), P("dp", "mp"), P("dp", "mp")),
        check_vma=False,
    )
```
